32 devices in a mesh: term: 4 (over y, x), sector: 8 (over z, core).
Axes of the slice: x: 2, y: 2, z: 4, core: 2. Of those that a mesh axis runs over, the one named last changes fastest.
Arguments:
- psi: bfloat16 [8, 8, 128, 128], P('sector'), may hold values from -6 to 6
- left_env: bfloat16 [8, 8, 128, 128], P('term', 'sector'), may hold values from -40 to 40
- right_env: bfloat16 [8, 8, 128, 128], P('term', 'sector'), may hold values from -4 to 4
- precond: bfloat16 [8, 8, 128, 128], P('sector'), may hold values from 0.5 to 4
- block_sizes: int32 [8], replicated, may hold values from 32 to 128, as said below
Outputs:
- state: bfloat16 [8, 8, 128, 128], P('sector')
- energy: float32 [3], replicated
The draws below stay inside these ranges and needn't reach their ends.
Inputs may be any that keep to these rules, and one draw needn't show every extreme that they name: `block_sizes`: some sector has exactly 128 rows in every draw.
All inputs are finite; a program needn't handle non-finite values.
Results may differ from the reference program's by a relative error of at most 0.022.
Values may be sent and summed in bfloat16 or wider, within the bound.
No kernel may reach another device: no remote copies, remote signals or barrier semaphores. Data moves between devices by JAX's collectives and lax.ppermute only.
A program may use at most 128 MiB of HBM per device.

```python
import math
import jax
import jax.numpy as jnp
from jax import lax

B = 128
K_DEV = 2
ITERS = 3
SEC = 8
TERMS = 8
N_TERM = 4


def draw_block_sizes(key, part):
    first_key, second_key = jax.random.split(jax.random.fold_in(key, 17))
    sizes = jax.random.randint(first_key, (SEC,), B // 4, B + 1)
    where = jax.random.randint(second_key, (), 0, SEC)
    return jnp.where(jnp.arange(SEC) == where, B, sizes).astype(jnp.int32)


def env_noise(key):
    return jnp.clip(jax.random.normal(key, (TERMS, SEC, B, B), jnp.float32), -4.0, 4.0)


def identity_blocks():
    rows = jnp.arange(B)
    return (rows[:, None] == rows[None, :]).astype(jnp.float32)[None, None]


def draw_left_env(key, part):
    noise = env_noise(jax.random.fold_in(key, 31))
    rise = 4.0
    position = jnp.arange(SEC).astype(jnp.float32) / max(SEC - 1, 1)
    scales = (rise ** position)[None, :, None, None]
    values = scales * (identity_blocks() + noise / B ** 0.5)
    return values.astype(jnp.bfloat16)


def draw_right_env(key, part):
    noise = env_noise(jax.random.fold_in(key, 47))
    rise = 4.0
    position = jnp.arange(SEC).astype(jnp.float32) / max(SEC - 1, 1)
    scales = (rise ** position)[None, :, None, None]
    values = 0.25 * scales * (identity_blocks() + noise / B ** 0.5)
    return values.astype(jnp.bfloat16)


def levels(stream_key, shape, cuts, smallest, top_value):
    loudness = 1.0
    for axis_at, blocks in cuts:
        draws = jax.random.uniform(jax.random.fold_in(jax.random.fold_in(stream_key, 6), axis_at), (blocks,), jnp.float32, smallest / len(cuts), top_value / len(cuts))
        loudness = loudness * jnp.repeat(jnp.exp(draws), shape[axis_at] // blocks).reshape((-1,) + (1,) * (len(shape) - 1 - axis_at))
    return loudness


def gaussian(own_key, dims, spread, reach, pieces=(), dtype=jnp.bfloat16):
    entries = jax.random.normal(own_key, dims, jnp.float32) * spread
    if len(pieces) > 0:
        entries = levels(own_key, dims, pieces, -0.22, 0.18) * entries
    return jnp.clip(entries, min=-reach, max=reach).astype(dtype)


def setup_inputs(seed: int = 0) -> dict:
    key_list = jax.random.split(jax.random.key(seed), 6)
    return {
        "psi": gaussian(key_list[0], (SEC, SEC, B, B), 1.0, 6.0, ((0, 8),)),
        "left_env": draw_left_env(jax.random.fold_in(key_list[5], 71), 0),
        "right_env": draw_right_env(jax.random.fold_in(key_list[5], 71), 0),
        "precond": jnp.clip(jnp.exp(math.log(4.0) - 2.0794415 * jax.random.uniform(key_list[3], (SEC, SEC, B, B), jnp.float32) ** levels(key_list[3], (SEC, SEC, B, B), ((0, 8),), -0.2, 0.2)), 0.5, 4.0).astype(jnp.bfloat16),
        "block_sizes": draw_block_sizes(jax.random.fold_in(key_list[5], 71), 0),
    }


def reference(psi, left_env, right_env, precond, block_sizes):
    rows = jnp.arange(B)
    valid = rows[None, :] < block_sizes[:, None]
    mask = (valid[:, None, :, None] & valid[None, :, None, :]).astype(jnp.float32)
    count = float(SEC * SEC * B * B)
    state = (psi.astype(jnp.float32) * mask).astype(jnp.bfloat16)
    scaling = precond.astype(jnp.float32)
    left_groups = left_env.reshape(N_TERM, K_DEV, SEC, B, B)
    right_groups = right_env.reshape(N_TERM, K_DEV, SEC, B, B)
    energies = []
    for step in range(ITERS):
        current = state.astype(jnp.float32)

        def group_sum(total, envs):

            def term_sum(acc, pair):
                left_term, right_term = pair
                images = jnp.einsum('ijab,jcb->ijac', current, right_term.astype(jnp.float32)).astype(jnp.bfloat16)
                images = lax.optimization_barrier(images)
                contrib = jnp.einsum('iac,ijcd->ijad', left_term.astype(jnp.float32), images.astype(jnp.float32))
                return (acc + contrib, None)
            acc, _ = lax.scan(term_sum, jnp.zeros((SEC, SEC, B, B), jnp.float32), envs)
            rounded = lax.optimization_barrier(acc.astype(jnp.bfloat16))
            return (total + rounded.astype(jnp.float32), None)
        total, _ = lax.scan(group_sum, jnp.zeros((SEC, SEC, B, B), jnp.float32), (left_groups, right_groups))
        image = total * mask
        theta = jnp.sum(current * image) / jnp.sum(current * current)
        fresh = current - (image - theta * current) / scaling
        squares = jnp.sum(fresh * fresh)
        state = (fresh * lax.rsqrt(squares / count + 1e-06)).astype(jnp.bfloat16)
        energies.append(theta)
    return (state, jnp.stack(energies))
```

```python
import functools

import jax
import jax.numpy as jnp
from jax import lax
from jax.experimental import pallas as pl
from jax.experimental.pallas import tpu as pltpu
from jax.sharding import PartitionSpec as P

EPS = 1e-06
SCALE = 2.0**-12
UNSCALE = 2.0**12
ROWS = 64
LANES = 128

POWERS = ((0, 0), (0, 1), (1, 0), (1, 1))
N0, E0 = 0, 1
N1, E1 = 2, 5
N2, E2 = 8, 17
N3 = 26


def split(x):
    high = x.astype(jnp.bfloat16)
    low = (x - high.astype(jnp.float32)).astype(jnp.bfloat16)
    return jnp.concatenate([high, low], axis=1)


def fold(x):
    return functools.reduce(lambda a, b: a + b, [x[r : r + 8] for r in range(0, x.shape[0], 8)])


def main_kernel(
    where_ref, sizes_ref, psi_ref, pre_ref, got_ref, swap_ref, gram_ref, basis_ref, left_cat, right_cat, sums
):
    groups, depth, width = swap_ref.shape[1], swap_ref.shape[2], swap_ref.shape[-1]
    owners = got_ref.shape[0]
    terms = owners * depth
    term, core, row = where_ref[0], where_ref[1], where_ref[2]
    own_size = sizes_ref[row]
    sums[...] = jnp.zeros_like(sums)
    for k in range(terms):
        left_cat[:, k * width : (k + 1) * width] = got_ref[k // depth, groups, k % depth]

    def apply(vectors):
        columns = []
        for b in range(2):
            stacked = jnp.concatenate(vectors[b], axis=0)
            inner = stacked.shape[1]
            images = lax.dot_general(
                stacked,
                right_cat[b, :, :inner],
                (((1,), (1,)), ((), ())),
                preferred_element_type=jnp.float32,
            ).astype(jnp.bfloat16)
            for n in range(len(vectors[b])):
                rows = images[n * width : (n + 1) * width]
                columns.append(
                    jnp.concatenate([rows[:, k * width : (k + 1) * width] for k in range(terms)], axis=0)
                )
        out = jnp.dot(left_cat[...], jnp.concatenate(columns, axis=1), preferred_element_type=jnp.float32)
        count = len(vectors[0])
        return [
            [out[:, (b * count + n) * width : (b * count + n + 1) * width] for n in range(count)]
            for b in range(2)
        ]

    def add(slot, value):
        sums[slot * 8 : slot * 8 + 8] += value

    def group(g):
        for k in range(terms):
            rows = slice(k * width, (k + 1) * width)
            for half in range(2):
                cols = slice(half * width, (half + 1) * width)
                right_cat[0, rows, cols] = got_ref[k // depth, g, k % depth]
                right_cat[1, rows, cols] = swap_ref[k // depth, g, k % depth]
        row_ids = lax.broadcasted_iota(jnp.int32, (width, width), 0)
        col_ids = lax.broadcasted_iota(jnp.int32, (width, width), 1)
        start, inverse = [], []
        for b in range(2):
            block = (term * groups + g) * 2 + (core if b == 0 else 1 - core)
            valid = (row_ids < own_size) & (col_ids < sizes_ref[block])
            start.append(jnp.where(valid, psi_ref[block].astype(jnp.float32), 0.0))
            inverse.append(jnp.where(valid, 1.0 / pre_ref[block].astype(jnp.float32), 0.0))

        images = apply([[s.astype(jnp.bfloat16)] for s in start])
        first = []
        for b in range(2):
            s, h, inv = start[b], images[b][0], inverse[b]
            add(N0, fold(s * s))
            add(E0, fold(s * h))
            first.append([SCALE * s - (SCALE * inv) * h, inv * s])

        images = apply([[split(x) for x in first[b]] for b in range(2)])
        second = []
        for b in range(2):
            inv = inverse[b]
            for m in range(2):
                for n in range(2):
                    if m <= n:
                        scale = 1.0 if m == n else 2.0
                        add(N1 + m + n, scale * fold(first[b][m] * first[b][n]))
                    add(E1 + m + n, fold(first[b][m] * images[b][n]))
            level = []
            for x, h in zip(first[b], images[b]):
                level += [SCALE * x - (SCALE * inv) * h, inv * x]
            second.append(level)

        images = apply([[split(x) for x in second[b]] for b in range(2)])
        for b in range(2):
            inv = inverse[b]
            third = []
            for x, h in zip(second[b], images[b]):
                third.append((SCALE * x - (SCALE * inv) * h, inv * x))
            for m in range(4):
                for d in range(2):
                    basis_ref[2 * m + d, 2 * g + b] = third[m][d]
            norm = [None] * 9
            energy = [None] * 9
            last = [None] * 27

            def put(table, at, value):
                table[at] = value if table[at] is None else table[at] + value

            for m in range(4):
                for n in range(4):
                    a0, a1 = POWERS[m][0] + POWERS[n][0], POWERS[m][1] + POWERS[n][1]
                    put(energy, 3 * a0 + a1, fold(second[b][m] * images[b][n]))
                    for d in range(2):
                        for e in range(2):
                            if (m, d) <= (n, e):
                                scale = 1.0 if (m, d) == (n, e) else 2.0
                                put(last, 9 * a0 + 3 * a1 + d + e, scale * fold(third[m][d] * third[n][e]))
                    if m <= n:
                        scale = 1.0 if m == n else 2.0
                        put(norm, 3 * a0 + a1, scale * fold(second[b][m] * second[b][n]))
            for at in range(9):
                add(N2 + at, norm[at])
                add(E2 + at, energy[at])
            for at in range(27):
                add(N3 + at, last[at])

    if groups == 1:
        group(0)
    else:

        @pl.loop(0, groups)
        def _(g):
            group(g)

    folded = functools.reduce(lambda a, b: a + b, [sums[pl.ds(s, ROWS, stride=8), :] for s in range(8)])
    totals = jnp.sum(folded, axis=1, keepdims=True)
    row_ids = lax.broadcasted_iota(jnp.int32, (ROWS, LANES), 0)
    col_ids = lax.broadcasted_iota(jnp.int32, (ROWS, LANES), 1)
    line = jnp.sum(jnp.where(row_ids == col_ids, totals, 0.0), axis=0, keepdims=True)
    gram_ref[...] = jnp.broadcast_to(line, gram_ref.shape)


def finish_kernel(count, where_ref, gram_ref, basis_ref, out_ref, energy_ref):
    core = where_ref[1]
    share = basis_ref.shape[1]
    gram = jnp.sum(gram_ref[...], axis=0, keepdims=True)
    lane = lax.broadcasted_iota(jnp.int32, (1, LANES), 1)

    def total(base, size, weight):
        inside = (lane >= base) & (lane < base + size)
        return jnp.sum(jnp.where(inside, gram * weight, 0.0), axis=1, keepdims=True)

    def power(exponent, value):
        return jnp.where(exponent == 0, 1.0, jnp.where(exponent == 1, value, value * value))

    theta0 = total(E0, 1, 1.0) / total(N0, 1, 1.0)
    tau0 = SCALE * theta0
    norm1 = total(N1, 3, power(lane - N1, tau0))
    theta1 = total(E1, 3, power(lane - E1, tau0)) / norm1
    tau1 = SCALE * theta1

    def weight2(base):
        at = lane - base
        return power(at // 3, tau0) * power(at % 3, tau1)

    norm2 = total(N2, 9, weight2(N2))
    theta2 = total(E2, 9, weight2(E2)) / norm2
    tau2 = SCALE * theta2
    at = lane - N3
    norm3 = total(N3, 27, power(at // 9, tau0) * power(at // 3 % 3, tau1) * power(at % 3, tau2))

    def factor(gain, norm):
        return lax.rsqrt(gain * gain * jnp.maximum(norm, 0.0) / count + EPS)

    gain = jnp.full((1, 1), UNSCALE, jnp.float32)
    gain = factor(gain, norm1) * gain * UNSCALE
    gain = factor(gain, norm2) * gain * UNSCALE
    gain = factor(gain, norm3) * gain
    weights = [gain, gain * tau1, gain * tau0, gain * tau0 * tau1]
    for at in range(share):
        even = at % 2 == 0
        value = None
        for m in range(4):
            part = weights[m] * (basis_ref[2 * m, at] + tau2 * basis_ref[2 * m + 1, at])
            value = part if value is None else value + part
        block = (at // 2) * 2 + (core if even else 1 - core)
        for t in range(out_ref.shape[0]):
            out_ref[t, block] = value.astype(jnp.bfloat16)
    energy_ref[...] = jnp.where(lane == 0, theta0, jnp.where(lane == 1, theta1, theta2))


def gather_chips(right_own, sectors):
    chips = sectors // 2
    if chips > 8:
        everything = lax.all_gather(right_own, "sector")
        everything = everything.reshape((chips, 2) + right_own.shape)
        return lax.dynamic_index_in_dim(everything, lax.axis_index("sector") % 2, 1, keepdims=False)
    pieces = [right_own]
    for shift in range(1, chips):
        moves = [(i, (i + 2 * shift) % sectors) for i in range(sectors)]
        pieces.append(lax.ppermute(right_own, "sector", moves))
    mine = lax.axis_index("sector") // 2
    stacked = jnp.stack(pieces[::-1] + pieces[:0:-1])
    return lax.dynamic_slice_in_dim(stacked, chips - 1 - mine, chips, 0)


def local(sectors, psi, left_env, right_env, precond, block_sizes):
    owners = lax.axis_size("term")
    devices = owners * sectors
    depth, width = right_env.shape[0], right_env.shape[-1]
    groups = sectors // 2 // owners
    share = 2 * groups
    own = lax.axis_index("sector")
    where = jnp.stack([lax.axis_index("term"), own % 2, own]).astype(jnp.int32)

    by_chip = gather_chips(right_env[:, 0], sectors)
    by_chip = by_chip.reshape(owners, groups, depth, width, width)
    left = jnp.broadcast_to(left_env[:, 0], (owners, 1, depth, width, width))
    got = lax.all_to_all(jnp.concatenate([by_chip, left], axis=1), "term", 0, 0)
    swap = lax.ppermute(got[:, :groups], "sector", [(i, i ^ 1) for i in range(sectors)])

    smem = pl.BlockSpec(memory_space=pltpu.SMEM)
    vmem = pl.BlockSpec(memory_space=pltpu.VMEM)
    terms = owners * depth
    gram, basis = pl.pallas_call(
        main_kernel,
        out_shape=(
            jax.ShapeDtypeStruct((devices, LANES), jnp.float32),
            jax.ShapeDtypeStruct((8, share, width, width), jnp.float32),
        ),
        in_specs=[smem, smem, vmem, vmem, vmem, vmem],
        out_specs=(vmem, vmem),
        scratch_shapes=[
            pltpu.VMEM((width, terms * width), jnp.bfloat16),
            pltpu.VMEM((2, terms * width, 2 * width), jnp.bfloat16),
            pltpu.VMEM((ROWS * 8, LANES), jnp.float32),
        ],
        compiler_params=pltpu.CompilerParams(vmem_limit_bytes=48 << 20),
        name="levels",
    )(where, block_sizes, psi[0], precond[0], got, swap)
    gram = lax.all_to_all(gram, ("term", "sector"), 0, 0, tiled=True)
    count = float(sectors * sectors * width * width)
    blocks, energy = pl.pallas_call(
        functools.partial(finish_kernel, count),
        out_shape=(
            jax.ShapeDtypeStruct((owners, share, width, width), jnp.bfloat16),
            jax.ShapeDtypeStruct((1, LANES), jnp.float32),
        ),
        in_specs=[smem, vmem, vmem],
        out_specs=(vmem, vmem),
        compiler_params=pltpu.CompilerParams(vmem_limit_bytes=48 << 20),
        name="finish",
    )(where, gram, basis)
    state = lax.all_to_all(blocks, "term", 0, 0)
    return (state.reshape((1, sectors, width, width)), energy[0, :3])


def solution(mesh):
    in_specs = (
        P("sector", None, None, None),
        P("term", "sector", None, None),
        P("term", "sector", None, None),
        P("sector", None, None, None),
        P(),
    )
    out_specs = (P("sector", None, None, None), P())
    return jax.shard_map(
        functools.partial(local, mesh.shape["sector"]),
        mesh=mesh,
        in_specs=in_specs,
        out_specs=out_specs,
        check_vma=False,
    )
```

```python
import functools

import jax
import jax.numpy as jnp
from jax import lax
from jax.experimental import pallas as pl
from jax.experimental.pallas import tpu as pltpu
from jax.sharding import PartitionSpec as P

EPS = 1e-06
SCALE = 2.0**-12
UNSCALE = 2.0**12
ROWS = 64
LANES = 128

POWERS = ((0, 0), (0, 1), (1, 0), (1, 1))
N0, E0 = 0, 1
N1, E1 = 2, 5
N2, E2 = 8, 17
N3 = 26


def split(x):
    high = x.astype(jnp.bfloat16)
    low = (x - high.astype(jnp.float32)).astype(jnp.bfloat16)
    return jnp.concatenate([high, low], axis=1)


def fold(x):
    return functools.reduce(lambda a, b: a + b, [x[r : r + 8] for r in range(0, x.shape[0], 8)])


def main_kernel(plan, sizes_ref, psi_ref, pre_ref, *refs):
    owners = plan.owners
    left_refs, own_refs, swap_refs = refs[:owners], refs[owners : 2 * owners], refs[2 * owners : 3 * owners]
    gram_ref, basis_ref, left_cat, right_cat, sums = refs[3 * owners :]
    groups, depth, width = own_refs[0].shape[0], own_refs[0].shape[1], own_refs[0].shape[-1]
    terms = owners * depth
    row = lax.axis_index("sector")
    core = row % 2
    chip = plan.first_chip(lax.axis_index("term"), row // 2)
    own_size = sizes_ref[row]
    sums[...] = jnp.zeros_like(sums)
    for k in range(terms):
        left_cat[:, k * width : (k + 1) * width] = left_refs[k // depth][k % depth]

    def apply(vectors):
        columns = []
        for b in range(2):
            stacked = jnp.concatenate(vectors[b], axis=0)
            inner = stacked.shape[1]
            images = lax.dot_general(
                stacked,
                right_cat[b, :, :inner],
                (((1,), (1,)), ((), ())),
                preferred_element_type=jnp.float32,
            ).astype(jnp.bfloat16)
            for n in range(len(vectors[b])):
                rows = images[n * width : (n + 1) * width]
                columns.append(
                    jnp.concatenate([rows[:, k * width : (k + 1) * width] for k in range(terms)], axis=0)
                )
        out = jnp.dot(left_cat[...], jnp.concatenate(columns, axis=1), preferred_element_type=jnp.float32)
        count = len(vectors[0])
        return [
            [out[:, (b * count + n) * width : (b * count + n + 1) * width] for n in range(count)]
            for b in range(2)
        ]

    def add(slot, value):
        sums[slot * 8 : slot * 8 + 8] += value

    def group(g):
        for k in range(terms):
            rows = slice(k * width, (k + 1) * width)
            for half in range(2):
                cols = slice(half * width, (half + 1) * width)
                right_cat[0, rows, cols] = own_refs[k // depth][g, k % depth]
                right_cat[1, rows, cols] = swap_refs[k // depth][g, k % depth]
        row_ids = lax.broadcasted_iota(jnp.int32, (width, width), 0)
        col_ids = lax.broadcasted_iota(jnp.int32, (width, width), 1)
        start, inverse = [], []
        for b in range(2):
            block = (chip + g) * 2 + (core if b == 0 else 1 - core)
            valid = (row_ids < own_size) & (col_ids < sizes_ref[block])
            start.append(jnp.where(valid, psi_ref[block].astype(jnp.float32), 0.0))
            inverse.append(jnp.where(valid, 1.0 / pre_ref[block].astype(jnp.float32), 0.0))

        images = apply([[s.astype(jnp.bfloat16)] for s in start])
        first = []
        for b in range(2):
            s, h, inv = start[b], images[b][0], inverse[b]
            add(N0, fold(s * s))
            add(E0, fold(s * h))
            first.append([SCALE * s - (SCALE * inv) * h, inv * s])

        images = apply([[split(x) for x in first[b]] for b in range(2)])
        second = []
        for b in range(2):
            inv = inverse[b]
            for m in range(2):
                for n in range(2):
                    if m <= n:
                        scale = 1.0 if m == n else 2.0
                        add(N1 + m + n, scale * fold(first[b][m] * first[b][n]))
                    add(E1 + m + n, fold(first[b][m] * images[b][n]))
            level = []
            for x, h in zip(first[b], images[b]):
                level += [SCALE * x - (SCALE * inv) * h, inv * x]
            second.append(level)

        images = apply([[split(x) for x in second[b]] for b in range(2)])
        for b in range(2):
            inv = inverse[b]
            third = []
            for x, h in zip(second[b], images[b]):
                third.append((SCALE * x - (SCALE * inv) * h, inv * x))
            for m in range(4):
                for d in range(2):
                    basis_ref[2 * m + d, 2 * g + b] = third[m][d]
            norm = [None] * 9
            energy = [None] * 9
            last = [None] * 27

            def put(table, at, value):
                table[at] = value if table[at] is None else table[at] + value

            for m in range(4):
                for n in range(4):
                    a0, a1 = POWERS[m][0] + POWERS[n][0], POWERS[m][1] + POWERS[n][1]
                    put(energy, 3 * a0 + a1, fold(second[b][m] * images[b][n]))
                    for d in range(2):
                        for e in range(2):
                            if (m, d) <= (n, e):
                                scale = 1.0 if (m, d) == (n, e) else 2.0
                                put(last, 9 * a0 + 3 * a1 + d + e, scale * fold(third[m][d] * third[n][e]))
                    if m <= n:
                        scale = 1.0 if m == n else 2.0
                        put(norm, 3 * a0 + a1, scale * fold(second[b][m] * second[b][n]))
            for at in range(9):
                add(N2 + at, norm[at])
                add(E2 + at, energy[at])
            for at in range(27):
                add(N3 + at, last[at])

    if groups == 1:
        group(0)
    else:

        @pl.loop(0, groups)
        def _(g):
            group(g)

    folded = functools.reduce(lambda a, b: a + b, [sums[pl.ds(s, ROWS, stride=8), :] for s in range(8)])
    totals = jnp.sum(folded, axis=1, keepdims=True)
    row_ids = lax.broadcasted_iota(jnp.int32, (ROWS, LANES), 0)
    col_ids = lax.broadcasted_iota(jnp.int32, (ROWS, LANES), 1)
    line = jnp.sum(jnp.where(row_ids == col_ids, totals, 0.0), axis=0, keepdims=True)
    gram_ref[...] = jnp.broadcast_to(line, gram_ref.shape)


def finish_kernel(count, gram_ref, basis_ref, out_ref, energy_ref):
    core = lax.axis_index("sector") % 2
    share = basis_ref.shape[1]
    gram = jnp.sum(gram_ref[...], axis=0, keepdims=True)
    lane = lax.broadcasted_iota(jnp.int32, (1, LANES), 1)

    def total(base, size, weight):
        inside = (lane >= base) & (lane < base + size)
        return jnp.sum(jnp.where(inside, gram * weight, 0.0), axis=1, keepdims=True)

    def power(exponent, value):
        return jnp.where(exponent == 0, 1.0, jnp.where(exponent == 1, value, value * value))

    theta0 = total(E0, 1, 1.0) / total(N0, 1, 1.0)
    tau0 = SCALE * theta0
    norm1 = total(N1, 3, power(lane - N1, tau0))
    theta1 = total(E1, 3, power(lane - E1, tau0)) / norm1
    tau1 = SCALE * theta1

    def weight2(base):
        at = lane - base
        return power(at // 3, tau0) * power(at % 3, tau1)

    norm2 = total(N2, 9, weight2(N2))
    theta2 = total(E2, 9, weight2(E2)) / norm2
    tau2 = SCALE * theta2
    at = lane - N3
    norm3 = total(N3, 27, power(at // 9, tau0) * power(at // 3 % 3, tau1) * power(at % 3, tau2))

    def factor(gain, norm):
        return lax.rsqrt(gain * gain * jnp.maximum(norm, 0.0) / count + EPS)

    gain = jnp.full((1, 1), UNSCALE, jnp.float32)
    gain = factor(gain, norm1) * gain * UNSCALE
    gain = factor(gain, norm2) * gain * UNSCALE
    gain = factor(gain, norm3) * gain
    weights = [gain, gain * tau1, gain * tau0, gain * tau0 * tau1]
    for at in range(share):
        even = at % 2 == 0
        value = None
        for m in range(4):
            part = weights[m] * (basis_ref[2 * m, at] + tau2 * basis_ref[2 * m + 1, at])
            value = part if value is None else value + part
        block = (at // 2) * 2 + (core if even else 1 - core)
        out_ref[block] = value.astype(jnp.bfloat16)
    energy_ref[...] = jnp.where(lane == 0, theta0, jnp.where(lane == 1, theta1, theta2))


def assemble_kernel(plan, *refs):
    pieces, out_ref, sems = refs[: plan.owners], refs[plan.owners], refs[plan.owners + 1]
    share = pieces[0].shape[0]
    term, chip = lax.axis_index("term"), lax.axis_index("sector") // 2
    copies = []
    for m in range(plan.owners):
        first = plan.first_chip(plan.hop(term, m), chip) * 2
        copies.append(pltpu.make_async_copy(pieces[m], out_ref.at[pl.ds(first, share)], sems.at[m]))
        copies[-1].start()
    for copy in copies:
        copy.wait()


class Plan:
    def __init__(self, owners, sectors):
        self.owners, self.sectors, self.chips = owners, sectors, sectors // 2
        self.groups = self.chips // owners
        self.direct = self.groups == 1
        if owners == 4:
            self.spread = ((0, 2, 1, 3), (1, 3, 0, 2), (2, 0, 3, 1), (3, 1, 2, 0))
        else:
            self.spread = tuple(tuple((q + t) % owners for q in range(owners)) for t in range(owners))

    def hop(self, term, offset):
        if self.owners & (self.owners - 1) == 0:
            return term ^ offset
        return (term + offset) % self.owners

    def back(self, offset):
        if self.owners & (self.owners - 1) == 0:
            return offset
        return (self.owners - offset) % self.owners

    def first_chip(self, term, chip):
        if not self.direct:
            return term * self.groups
        found = jnp.int32(0)
        for t in range(self.owners):
            for q in range(self.owners):
                hit = (term == t) & (chip == self.spread[t][q])
                found = jnp.where(hit, q, found)
        return found


def from_owner(plan, value, offset):
    if offset == 0:
        return value
    moves = [(plan.hop(t, offset), t) for t in range(plan.owners)]
    return lax.ppermute(value, "term", moves)


def inputs(plan, left, right):
    sectors, owners, groups = plan.sectors, plan.owners, plan.groups
    cores = [(i, i ^ 1) for i in range(sectors)]
    if plan.direct:
        lefts = [from_owner(plan, left, m) for m in range(owners)]
        own = []
        for m in range(owners):
            moves = []
            for t in range(owners):
                for q in range(plan.chips):
                    for c in range(2):
                        source = plan.hop(t, m) * sectors + 2 * q + c
                        moves.append((source, t * sectors + 2 * plan.spread[t][q] + c))
            own.append(lax.ppermute(right, ("term", "sector"), moves)[None])
        swapped = [lax.ppermute(x, "sector", cores) for x in own]
        return lefts, own, swapped
    everything = lax.all_gather(right, "sector").reshape((owners, groups, 2) + right.shape)
    by_chip = lax.dynamic_index_in_dim(everything, lax.axis_index("sector") % 2, 2, keepdims=False)
    spread_left = jnp.broadcast_to(left, (owners, 1) + left.shape)
    got = lax.all_to_all(jnp.concatenate([by_chip, spread_left], axis=1), "term", 0, 0)
    swapped = lax.ppermute(got[:, :groups], "sector", cores)
    lefts = [got[t, groups] for t in range(owners)]
    own = [got[t, :groups] for t in range(owners)]
    return lefts, own, [swapped[t] for t in range(owners)]


def local(plan, psi, left_env, right_env, precond, block_sizes):
    owners, sectors = plan.owners, plan.sectors
    devices = owners * sectors
    depth, width = right_env.shape[0], right_env.shape[-1]
    share = 2 * plan.groups
    lefts, own, swapped = inputs(plan, left_env[:, 0], right_env[:, 0])

    smem = pl.BlockSpec(memory_space=pltpu.SMEM)
    vmem = pl.BlockSpec(memory_space=pltpu.VMEM)
    terms = owners * depth
    gram, basis = pl.pallas_call(
        functools.partial(main_kernel, plan),
        out_shape=(
            jax.ShapeDtypeStruct((devices, LANES), jnp.float32),
            jax.ShapeDtypeStruct((8, share, width, width), jnp.float32),
        ),
        in_specs=[smem] + [vmem] * (2 + 3 * owners),
        out_specs=(vmem, vmem),
        scratch_shapes=[
            pltpu.VMEM((width, terms * width), jnp.bfloat16),
            pltpu.VMEM((2, terms * width, 2 * width), jnp.bfloat16),
            pltpu.VMEM((ROWS * 8, LANES), jnp.float32),
        ],
        compiler_params=pltpu.CompilerParams(vmem_limit_bytes=48 << 20),
        name="levels",
    )(block_sizes, psi[0], precond[0], *lefts, *own, *swapped)
    gram = lax.all_to_all(gram, ("term", "sector"), 0, 0, tiled=True)
    count = float(sectors * sectors * width * width)
    blocks, energy = pl.pallas_call(
        functools.partial(finish_kernel, count),
        out_shape=(
            jax.ShapeDtypeStruct((share, width, width), jnp.bfloat16),
            jax.ShapeDtypeStruct((1, LANES), jnp.float32),
        ),
        in_specs=[vmem, vmem],
        out_specs=(vmem, vmem),
        compiler_params=pltpu.CompilerParams(vmem_limit_bytes=48 << 20),
        name="finish",
    )(gram, basis)
    anywhere = pl.BlockSpec(memory_space=pl.ANY)
    state = pl.pallas_call(
        functools.partial(assemble_kernel, plan),
        out_shape=jax.ShapeDtypeStruct((sectors, width, width), jnp.bfloat16),
        in_specs=[anywhere] * owners,
        out_specs=anywhere,
        scratch_shapes=[pltpu.SemaphoreType.DMA((owners,))],
        name="assemble",
    )(*[from_owner(plan, blocks, m) for m in range(owners)])
    return (state[None], energy[0, :3])


def solution(mesh):
    in_specs = (
        P("sector", None, None, None),
        P("term", "sector", None, None),
        P("term", "sector", None, None),
        P("sector", None, None, None),
        P(),
    )
    out_specs = (P("sector", None, None, None), P())
    return jax.shard_map(
        functools.partial(local, Plan(mesh.shape["term"], mesh.shape["sector"])),
        mesh=mesh,
        in_specs=in_specs,
        out_specs=out_specs,
        check_vma=False,
    )
```

```python
import functools

import jax
import jax.numpy as jnp
from jax import lax
from jax.experimental import pallas as pl
from jax.experimental.pallas import tpu as pltpu
from jax.sharding import PartitionSpec as P

EPS = 1e-06
SCALE = 2.0**-12
UNSCALE = 2.0**12
ROWS = 64
LANES = 128

POWERS = ((0, 0), (0, 1), (1, 0), (1, 1))
N0, E0 = 0, 1
N1, E1 = 2, 5
N2, E2 = 8, 17
N3 = 26


def split(x):
    high = x.astype(jnp.bfloat16)
    low = (x - high.astype(jnp.float32)).astype(jnp.bfloat16)
    return jnp.concatenate([high, low], axis=1)


def fold(x):
    return functools.reduce(lambda a, b: a + b, [x[r : r + 8] for r in range(0, x.shape[0], 8)])


def main_kernel(plan, sizes_hbm, psi_hbm, pre_hbm, left_hbm, *refs):
    owners = plan.owners
    left_refs, refs = refs[: owners - 1], refs[owners - 1 :]
    own_refs, swap_refs, refs = refs[:owners], refs[owners : 2 * owners], refs[2 * owners :]
    gram_ref, basis_ref, sizes_ref, psi_ref, pre_ref, own_left, left_cat, right_cat, sums, sems = refs
    groups, depth, width = own_refs[0].shape[0], own_refs[0].shape[1], own_refs[0].shape[-1]
    terms = owners * depth
    row = lax.axis_index("sector")
    core = row % 2
    chip = plan.first_chip(lax.axis_index("term"), row // 2)
    blocks = pl.ds(2 * chip, psi_ref.shape[0])
    copies = [
        pltpu.make_async_copy(sizes_hbm, sizes_ref, sems.at[0]),
        pltpu.make_async_copy(psi_hbm.at[blocks], psi_ref, sems.at[1]),
        pltpu.make_async_copy(pre_hbm.at[blocks], pre_ref, sems.at[2]),
        pltpu.make_async_copy(left_hbm, own_left, sems.at[3]),
    ]
    for copy in copies:
        copy.start()
    sums[...] = jnp.zeros_like(sums)
    for k in range(depth, terms):
        left_cat[:, k * width : (k + 1) * width] = left_refs[k // depth - 1][k % depth]

    def finish_copies():
        for copy in copies:
            copy.wait()
        for k in range(depth):
            left_cat[:, k * width : (k + 1) * width] = own_left[k]

    def apply(vectors):
        columns = []
        for b in range(2):
            stacked = jnp.concatenate(vectors[b], axis=0)
            inner = stacked.shape[1]
            images = lax.dot_general(
                stacked,
                right_cat[b, :, :inner],
                (((1,), (1,)), ((), ())),
                preferred_element_type=jnp.float32,
            ).astype(jnp.bfloat16)
            for n in range(len(vectors[b])):
                rows = images[n * width : (n + 1) * width]
                columns.append(
                    jnp.concatenate([rows[:, k * width : (k + 1) * width] for k in range(terms)], axis=0)
                )
        out = jnp.dot(left_cat[...], jnp.concatenate(columns, axis=1), preferred_element_type=jnp.float32)
        count = len(vectors[0])
        return [
            [out[:, (b * count + n) * width : (b * count + n + 1) * width] for n in range(count)]
            for b in range(2)
        ]

    def add(slot, value):
        sums[slot * 8 : slot * 8 + 8] += value

    def group(g):
        for k in range(terms):
            rows = slice(k * width, (k + 1) * width)
            for half in range(2):
                cols = slice(half * width, (half + 1) * width)
                right_cat[0, rows, cols] = own_refs[k // depth][g, k % depth]
                right_cat[1, rows, cols] = swap_refs[k // depth][g, k % depth]
        if groups == 1:
            finish_copies()
        row_ids = lax.broadcasted_iota(jnp.int32, (width, width), 0)
        col_ids = lax.broadcasted_iota(jnp.int32, (width, width), 1)
        start, inverse = [], []
        for b in range(2):
            block = 2 * g + (core if b == 0 else 1 - core)
            valid = (row_ids < sizes_ref[row]) & (col_ids < sizes_ref[2 * chip + block])
            start.append(jnp.where(valid, psi_ref[block].astype(jnp.float32), 0.0))
            inverse.append(jnp.where(valid, 1.0 / pre_ref[block].astype(jnp.float32), 0.0))

        images = apply([[s.astype(jnp.bfloat16)] for s in start])
        first = []
        for b in range(2):
            s, h, inv = start[b], images[b][0], inverse[b]
            add(N0, fold(s * s))
            add(E0, fold(s * h))
            first.append([SCALE * s - (SCALE * inv) * h, inv * s])

        images = apply([[split(x) for x in first[b]] for b in range(2)])
        second = []
        for b in range(2):
            inv = inverse[b]
            for m in range(2):
                for n in range(2):
                    if m <= n:
                        scale = 1.0 if m == n else 2.0
                        add(N1 + m + n, scale * fold(first[b][m] * first[b][n]))
                    add(E1 + m + n, fold(first[b][m] * images[b][n]))
            level = []
            for x, h in zip(first[b], images[b]):
                level += [SCALE * x - (SCALE * inv) * h, inv * x]
            second.append(level)

        images = apply([[split(x) for x in second[b]] for b in range(2)])
        for b in range(2):
            inv = inverse[b]
            third = []
            for x, h in zip(second[b], images[b]):
                third.append((SCALE * x - (SCALE * inv) * h, inv * x))
            for m in range(4):
                for d in range(2):
                    basis_ref[2 * m + d, 2 * g + b] = third[m][d]
            norm = [None] * 9
            energy = [None] * 9
            last = [None] * 27

            def put(table, at, value):
                table[at] = value if table[at] is None else table[at] + value

            for m in range(4):
                for n in range(4):
                    a0, a1 = POWERS[m][0] + POWERS[n][0], POWERS[m][1] + POWERS[n][1]
                    put(energy, 3 * a0 + a1, fold(second[b][m] * images[b][n]))
                    for d in range(2):
                        for e in range(2):
                            if (m, d) <= (n, e):
                                scale = 1.0 if (m, d) == (n, e) else 2.0
                                put(last, 9 * a0 + 3 * a1 + d + e, scale * fold(third[m][d] * third[n][e]))
                    if m <= n:
                        scale = 1.0 if m == n else 2.0
                        put(norm, 3 * a0 + a1, scale * fold(second[b][m] * second[b][n]))
            for at in range(9):
                add(N2 + at, norm[at])
                add(E2 + at, energy[at])
            for at in range(27):
                add(N3 + at, last[at])

    if groups == 1:
        group(0)
    else:
        finish_copies()

        @pl.loop(0, groups)
        def _(g):
            group(g)

    folded = functools.reduce(lambda a, b: a + b, [sums[pl.ds(s, ROWS, stride=8), :] for s in range(8)])
    totals = jnp.sum(folded, axis=1, keepdims=True)
    row_ids = lax.broadcasted_iota(jnp.int32, (ROWS, LANES), 0)
    col_ids = lax.broadcasted_iota(jnp.int32, (ROWS, LANES), 1)
    line = jnp.sum(jnp.where(row_ids == col_ids, totals, 0.0), axis=0, keepdims=True)
    gram_ref[...] = jnp.broadcast_to(line, gram_ref.shape)


def finish_kernel(count, gram_ref, basis_ref, out_ref, energy_ref):
    core = lax.axis_index("sector") % 2
    share = basis_ref.shape[1]
    gram = jnp.sum(gram_ref[...], axis=0, keepdims=True)
    lane = lax.broadcasted_iota(jnp.int32, (1, LANES), 1)

    def total(base, size, weight):
        inside = (lane >= base) & (lane < base + size)
        return jnp.sum(jnp.where(inside, gram * weight, 0.0), axis=1, keepdims=True)

    def power(exponent, value):
        return jnp.where(exponent == 0, 1.0, jnp.where(exponent == 1, value, value * value))

    theta0 = total(E0, 1, 1.0) / total(N0, 1, 1.0)
    tau0 = SCALE * theta0
    norm1 = total(N1, 3, power(lane - N1, tau0))
    theta1 = total(E1, 3, power(lane - E1, tau0)) / norm1
    tau1 = SCALE * theta1

    def weight2(base):
        at = lane - base
        return power(at // 3, tau0) * power(at % 3, tau1)

    norm2 = total(N2, 9, weight2(N2))
    theta2 = total(E2, 9, weight2(E2)) / norm2
    tau2 = SCALE * theta2
    at = lane - N3
    norm3 = total(N3, 27, power(at // 9, tau0) * power(at // 3 % 3, tau1) * power(at % 3, tau2))

    def factor(gain, norm):
        return lax.rsqrt(gain * gain * jnp.maximum(norm, 0.0) / count + EPS)

    gain = jnp.full((1, 1), UNSCALE, jnp.float32)
    gain = factor(gain, norm1) * gain * UNSCALE
    gain = factor(gain, norm2) * gain * UNSCALE
    gain = factor(gain, norm3) * gain
    weights = [gain, gain * tau1, gain * tau0, gain * tau0 * tau1]
    for at in range(share):
        even = at % 2 == 0
        value = None
        for m in range(4):
            part = weights[m] * (basis_ref[2 * m, at] + tau2 * basis_ref[2 * m + 1, at])
            value = part if value is None else value + part
        block = (at // 2) * 2 + (core if even else 1 - core)
        out_ref[block] = value.astype(jnp.bfloat16)
    energy_ref[...] = jnp.where(lane == 0, theta0, jnp.where(lane == 1, theta1, theta2))


def assemble_kernel(plan, *refs):
    pieces, out_ref, sems = refs[: plan.owners], refs[plan.owners], refs[plan.owners + 1]
    share = pieces[0].shape[0]
    term, chip = lax.axis_index("term"), lax.axis_index("sector") // 2
    copies = []
    for m in range(plan.owners):
        first = plan.first_chip(plan.hop(term, m), chip) * 2
        copies.append(pltpu.make_async_copy(pieces[m], out_ref.at[pl.ds(first, share)], sems.at[m]))
        copies[-1].start()
    for copy in copies:
        copy.wait()


class Plan:
    def __init__(self, owners, sectors):
        self.owners, self.sectors, self.chips = owners, sectors, sectors // 2
        self.groups = self.chips // owners
        self.direct = self.groups == 1
        if owners == 4:
            self.spread = ((0, 2, 1, 3), (1, 3, 0, 2), (2, 0, 3, 1), (3, 1, 2, 0))
        else:
            self.spread = tuple(tuple((q + t) % owners for q in range(owners)) for t in range(owners))

    def hop(self, term, offset):
        if self.owners & (self.owners - 1) == 0:
            return term ^ offset
        return (term + offset) % self.owners

    def back(self, offset):
        if self.owners & (self.owners - 1) == 0:
            return offset
        return (self.owners - offset) % self.owners

    def first_chip(self, term, chip):
        if not self.direct:
            return term * self.groups
        found = jnp.int32(0)
        for t in range(self.owners):
            for q in range(self.owners):
                hit = (term == t) & (chip == self.spread[t][q])
                found = jnp.where(hit, q, found)
        return found


def from_owner(plan, value, offset):
    if offset == 0:
        return value
    moves = [(plan.hop(t, offset), t) for t in range(plan.owners)]
    return lax.ppermute(value, "term", moves)


def inputs(plan, left, right):
    sectors, owners, groups = plan.sectors, plan.owners, plan.groups
    cores = [(i, i ^ 1) for i in range(sectors)]
    if plan.direct:
        lefts = [from_owner(plan, left, m) for m in range(owners)]
        own = []
        for m in range(owners):
            moves = []
            for t in range(owners):
                for q in range(plan.chips):
                    for c in range(2):
                        source = plan.hop(t, m) * sectors + 2 * q + c
                        moves.append((source, t * sectors + 2 * plan.spread[t][q] + c))
            own.append(lax.ppermute(right, ("term", "sector"), moves)[None])
        swapped = [lax.ppermute(x, "sector", cores) for x in own]
        return lefts, own, swapped
    everything = lax.all_gather(right, "sector").reshape((owners, groups, 2) + right.shape)
    by_chip = lax.dynamic_index_in_dim(everything, lax.axis_index("sector") % 2, 2, keepdims=False)
    spread_left = jnp.broadcast_to(left, (owners, 1) + left.shape)
    got = lax.all_to_all(jnp.concatenate([by_chip, spread_left], axis=1), "term", 0, 0)
    swapped = lax.ppermute(got[:, :groups], "sector", cores)
    lefts = [got[t, groups] for t in range(owners)]
    own = [got[t, :groups] for t in range(owners)]
    return lefts, own, [swapped[t] for t in range(owners)]


def local(plan, psi, left_env, right_env, precond, block_sizes):
    owners, sectors = plan.owners, plan.sectors
    devices = owners * sectors
    depth, width = right_env.shape[0], right_env.shape[-1]
    share = 2 * plan.groups
    lefts, own, swapped = inputs(plan, left_env[:, 0], right_env[:, 0])

    anywhere = pl.BlockSpec(memory_space=pltpu.HBM)
    vmem = pl.BlockSpec(memory_space=pltpu.VMEM)
    parked = [
        pltpu.with_memory_space_constraint(x, pltpu.HBM) for x in (block_sizes, psi[0], precond[0], lefts[0])
    ]
    terms = owners * depth
    gram, basis = pl.pallas_call(
        functools.partial(main_kernel, plan),
        out_shape=(
            jax.ShapeDtypeStruct((devices, LANES), jnp.float32),
            jax.ShapeDtypeStruct((8, share, width, width), jnp.float32),
        ),
        in_specs=[anywhere] * 4 + [vmem] * (3 * owners - 1),
        out_specs=(vmem, vmem),
        scratch_shapes=[
            pltpu.SMEM((sectors,), jnp.int32),
            pltpu.VMEM((share, width, width), jnp.bfloat16),
            pltpu.VMEM((share, width, width), jnp.bfloat16),
            pltpu.VMEM((depth, width, width), jnp.bfloat16),
            pltpu.VMEM((width, terms * width), jnp.bfloat16),
            pltpu.VMEM((2, terms * width, 2 * width), jnp.bfloat16),
            pltpu.VMEM((ROWS * 8, LANES), jnp.float32),
            pltpu.SemaphoreType.DMA((4,)),
        ],
        compiler_params=pltpu.CompilerParams(vmem_limit_bytes=48 << 20),
        name="levels",
    )(*parked, *lefts[1:], *own, *swapped)
    gram = lax.all_to_all(gram, ("term", "sector"), 0, 0, tiled=True)
    count = float(sectors * sectors * width * width)
    blocks, energy = pl.pallas_call(
        functools.partial(finish_kernel, count),
        out_shape=(
            jax.ShapeDtypeStruct((share, width, width), jnp.bfloat16),
            jax.ShapeDtypeStruct((1, LANES), jnp.float32),
        ),
        in_specs=[vmem, vmem],
        out_specs=(vmem, vmem),
        compiler_params=pltpu.CompilerParams(vmem_limit_bytes=48 << 20),
        name="finish",
    )(gram, basis)
    state = pl.pallas_call(
        functools.partial(assemble_kernel, plan),
        out_shape=jax.ShapeDtypeStruct((sectors, width, width), jnp.bfloat16),
        in_specs=[vmem] * owners,
        out_specs=anywhere,
        scratch_shapes=[pltpu.SemaphoreType.DMA((owners,))],
        compiler_params=pltpu.CompilerParams(vmem_limit_bytes=16 << 20),
        name="assemble",
    )(*[from_owner(plan, blocks, m) for m in range(owners)])
    return (state[None], energy[0, :3])


def solution(mesh):
    in_specs = (
        P("sector", None, None, None),
        P("term", "sector", None, None),
        P("term", "sector", None, None),
        P("sector", None, None, None),
        P(),
    )
    out_specs = (P("sector", None, None, None), P())
    return jax.shard_map(
        functools.partial(local, Plan(mesh.shape["term"], mesh.shape["sector"])),
        mesh=mesh,
        in_specs=in_specs,
        out_specs=out_specs,
        check_vma=False,
    )
```

```python
import functools

import jax
import jax.numpy as jnp
from jax import lax
from jax.experimental import pallas as pl
from jax.experimental.pallas import tpu as pltpu
from jax.sharding import PartitionSpec as P

EPS = 1e-06
SCALE = 2.0**-12
UNSCALE = 2.0**12
ROWS = 64
LANES = 128

POWERS = ((0, 0), (0, 1), (1, 0), (1, 1))
N0, E0 = 0, 1
N1, E1 = 2, 5
N2, E2 = 8, 17
N3 = 26


def split(x):
    high = x.astype(jnp.bfloat16)
    low = (x - high.astype(jnp.float32)).astype(jnp.bfloat16)
    return jnp.concatenate([high, low], axis=1)


def fold(x):
    return functools.reduce(lambda a, b: a + b, [x[r : r + 8] for r in range(0, x.shape[0], 8)])


def stack_right(right_cat, right_refs, g, depth, width):
    for k in range(len(right_refs) * depth):
        for half in range(2):
            right_cat[k * width : (k + 1) * width, half * width : (half + 1) * width] = right_refs[k // depth][
                g, k % depth
            ]


def levels(left_cat, right_cat, sums, basis_ref, g, start, inv):
    width = start.shape[0]
    terms = left_cat.shape[1] // width

    def apply(vectors):
        stacked = jnp.concatenate(vectors, axis=0)
        images = lax.dot_general(
            stacked,
            right_cat[:, : stacked.shape[1]],
            (((1,), (1,)), ((), ())),
            preferred_element_type=jnp.float32,
        ).astype(jnp.bfloat16)
        columns = []
        for n in range(len(vectors)):
            rows = images[n * width : (n + 1) * width]
            columns.append(jnp.concatenate([rows[:, k * width : (k + 1) * width] for k in range(terms)], axis=0))
        out = jnp.dot(left_cat[...], jnp.concatenate(columns, axis=1), preferred_element_type=jnp.float32)
        return [out[:, n * width : (n + 1) * width] for n in range(len(vectors))]

    def add(slot, value):
        sums[slot * 8 : slot * 8 + 8] += value

    def put(table, at, value):
        table[at] = value if table[at] is None else table[at] + value

    def advance(vectors, images):
        level = []
        for x, h in zip(vectors, images):
            level += [SCALE * x - (SCALE * inv) * h, inv * x]
        return level

    (image,) = apply([start])
    state = start.astype(jnp.float32)
    add(N0, fold(state * state))
    add(E0, fold(state * image))
    first = advance([state], [image])

    images = apply([split(x) for x in first])
    for m in range(2):
        for n in range(2):
            if m <= n:
                add(N1 + m + n, (1.0 if m == n else 2.0) * fold(first[m] * first[n]))
            add(E1 + m + n, fold(first[m] * images[n]))
    second = advance(first, images)

    images = apply([split(x) for x in second])
    third = advance(second, images)
    for m in range(8):
        basis_ref[m, g] = third[m]
    norm, energy, last = [None] * 9, [None] * 9, [None] * 27
    for m in range(4):
        for n in range(4):
            a0, a1 = POWERS[m][0] + POWERS[n][0], POWERS[m][1] + POWERS[n][1]
            put(energy, 3 * a0 + a1, fold(second[m] * images[n]))
            if m <= n:
                put(norm, 3 * a0 + a1, (1.0 if m == n else 2.0) * fold(second[m] * second[n]))
            for d in range(2):
                for e in range(2):
                    if (m, d) <= (n, e):
                        scale = 1.0 if (m, d) == (n, e) else 2.0
                        put(last, 9 * a0 + 3 * a1 + d + e, scale * fold(third[2 * m + d] * third[2 * n + e]))
    for at in range(9):
        add(N2 + at, norm[at])
        add(E2 + at, energy[at])
    for at in range(27):
        add(N3 + at, last[at])


def each_group(groups, body):
    if groups == 1:
        body(0)
    else:
        pl.loop(0, groups)(body)


def own_kernel(plan, sizes_hbm, psi_hbm, pre_hbm, left_hbm, *refs):
    owners, groups = plan.owners, plan.groups
    left_refs, right_refs, refs = refs[: owners - 1], refs[owners - 1 : 2 * owners - 1], refs[2 * owners - 1 :]
    left_cat, start_ref, inverse_ref, sums, basis_ref = refs[:5]
    sizes_ref, psi_ref, pre_ref, own_left, right_cat, sems = refs[5:]
    depth, width = own_left.shape[0], own_left.shape[-1]
    terms = owners * depth
    row = lax.axis_index("sector")
    core = row % 2
    chip = plan.first_chip(lax.axis_index("term"), row // 2)
    blocks = pl.ds(2 * chip, psi_ref.shape[0])
    copies = [
        pltpu.make_async_copy(sizes_hbm, sizes_ref, sems.at[0]),
        pltpu.make_async_copy(psi_hbm.at[blocks], psi_ref, sems.at[1]),
        pltpu.make_async_copy(pre_hbm.at[blocks], pre_ref, sems.at[2]),
        pltpu.make_async_copy(left_hbm, own_left, sems.at[3]),
    ]
    for copy in copies:
        copy.start()
    sums[...] = jnp.zeros_like(sums)
    for k in range(depth, terms):
        left_cat[:, k * width : (k + 1) * width] = left_refs[k // depth - 1][k % depth]
    if groups == 1:
        stack_right(right_cat, right_refs, 0, depth, width)
    for copy in copies:
        copy.wait()
    for k in range(depth):
        left_cat[:, k * width : (k + 1) * width] = own_left[k]

    def body(g):
        row_ids = lax.broadcasted_iota(jnp.int32, (width, width), 0)
        col_ids = lax.broadcasted_iota(jnp.int32, (width, width), 1)
        if groups > 1:
            stack_right(right_cat, right_refs, g, depth, width)

        def masked(block):
            valid = (row_ids < sizes_ref[row]) & (col_ids < sizes_ref[2 * chip + block])
            start = jnp.where(valid, psi_ref[block].astype(jnp.float32), 0.0).astype(jnp.bfloat16)
            return start, jnp.where(valid, 1.0 / pre_ref[block].astype(jnp.float32), 0.0)

        start, inverse = masked(2 * g + core)
        levels(left_cat, right_cat, sums, basis_ref, g, start, inverse)
        start_ref[g], inverse_ref[g] = masked(2 * g + 1 - core)

    each_group(groups, body)


def other_kernel(plan, left_cat, start_ref, inverse_ref, sums_in, *refs):
    right_refs, (gram_ref, basis_ref, sums, right_cat) = refs[: plan.owners], refs[plan.owners :]
    depth, width = right_refs[0].shape[1], right_refs[0].shape[-1]
    sums[...] = sums_in[...]

    def body(g):
        stack_right(right_cat, right_refs, g, depth, width)
        levels(left_cat, right_cat, sums, basis_ref, g, start_ref[g], inverse_ref[g])

    each_group(plan.groups, body)
    folded = functools.reduce(lambda a, b: a + b, [sums[pl.ds(s, ROWS, stride=8), :] for s in range(8)])
    totals = jnp.sum(folded, axis=1, keepdims=True)
    row_ids = lax.broadcasted_iota(jnp.int32, (ROWS, LANES), 0)
    col_ids = lax.broadcasted_iota(jnp.int32, (ROWS, LANES), 1)
    line = jnp.sum(jnp.where(row_ids == col_ids, totals, 0.0), axis=0, keepdims=True)
    gram_ref[...] = jnp.broadcast_to(line, gram_ref.shape)


def finish_kernel(count, gram_ref, own_ref, other_ref, out_ref, energy_ref):
    core = lax.axis_index("sector") % 2
    share = out_ref.shape[0]
    gram = jnp.sum(gram_ref[...], axis=0, keepdims=True)
    lane = lax.broadcasted_iota(jnp.int32, (1, LANES), 1)

    def total(base, size, weight):
        inside = (lane >= base) & (lane < base + size)
        return jnp.sum(jnp.where(inside, gram * weight, 0.0), axis=1, keepdims=True)

    def power(exponent, value):
        return jnp.where(exponent == 0, 1.0, jnp.where(exponent == 1, value, value * value))

    theta0 = total(E0, 1, 1.0) / total(N0, 1, 1.0)
    tau0 = SCALE * theta0
    norm1 = total(N1, 3, power(lane - N1, tau0))
    theta1 = total(E1, 3, power(lane - E1, tau0)) / norm1
    tau1 = SCALE * theta1

    def weight2(base):
        at = lane - base
        return power(at // 3, tau0) * power(at % 3, tau1)

    norm2 = total(N2, 9, weight2(N2))
    theta2 = total(E2, 9, weight2(E2)) / norm2
    tau2 = SCALE * theta2
    at = lane - N3
    norm3 = total(N3, 27, power(at // 9, tau0) * power(at // 3 % 3, tau1) * power(at % 3, tau2))

    def factor(gain, norm):
        return lax.rsqrt(gain * gain * jnp.maximum(norm, 0.0) / count + EPS)

    gain = jnp.full((1, 1), UNSCALE, jnp.float32)
    gain = factor(gain, norm1) * gain * UNSCALE
    gain = factor(gain, norm2) * gain * UNSCALE
    gain = factor(gain, norm3) * gain
    weights = [gain, gain * tau1, gain * tau0, gain * tau0 * tau1]
    for at in range(share):
        even, basis_ref = (True, own_ref) if at % 2 == 0 else (False, other_ref)
        value = None
        for m in range(4):
            part = weights[m] * (basis_ref[2 * m, at // 2] + tau2 * basis_ref[2 * m + 1, at // 2])
            value = part if value is None else value + part
        block = (at // 2) * 2 + (core if even else 1 - core)
        out_ref[block] = value.astype(jnp.bfloat16)
    energy_ref[...] = jnp.where(lane == 0, theta0, jnp.where(lane == 1, theta1, theta2))


def assemble_kernel(plan, *refs):
    pieces, out_ref, sems = refs[: plan.owners], refs[plan.owners], refs[plan.owners + 1]
    share = pieces[0].shape[0]
    term, chip = lax.axis_index("term"), lax.axis_index("sector") // 2
    copies = []
    for m in range(plan.owners):
        first = plan.first_chip(plan.hop(term, m), chip) * 2
        copies.append(pltpu.make_async_copy(pieces[m], out_ref.at[pl.ds(first, share)], sems.at[m]))
        copies[-1].start()
    for copy in copies:
        copy.wait()


class Plan:
    def __init__(self, owners, sectors):
        self.owners, self.sectors, self.chips = owners, sectors, sectors // 2
        self.groups = self.chips // owners
        self.direct = self.groups == 1
        if owners == 4:
            self.spread = ((0, 2, 1, 3), (1, 3, 0, 2), (2, 0, 3, 1), (3, 1, 2, 0))
        else:
            self.spread = tuple(tuple((q + t) % owners for q in range(owners)) for t in range(owners))

    def hop(self, term, offset):
        if self.owners & (self.owners - 1) == 0:
            return term ^ offset
        return (term + offset) % self.owners

    def back(self, offset):
        if self.owners & (self.owners - 1) == 0:
            return offset
        return (self.owners - offset) % self.owners

    def first_chip(self, term, chip):
        if not self.direct:
            return term * self.groups
        found = jnp.int32(0)
        for t in range(self.owners):
            for q in range(self.owners):
                hit = (term == t) & (chip == self.spread[t][q])
                found = jnp.where(hit, q, found)
        return found


def from_owner(plan, value, offset):
    if offset == 0:
        return value
    moves = [(plan.hop(t, offset), t) for t in range(plan.owners)]
    return lax.ppermute(value, "term", moves)


def inputs(plan, left, right):
    sectors, owners, groups = plan.sectors, plan.owners, plan.groups
    cores = [(i, i ^ 1) for i in range(sectors)]
    if plan.direct:
        lefts = [from_owner(plan, left, m) for m in range(owners)]
        own = []
        for m in range(owners):
            moves = []
            for t in range(owners):
                for q in range(plan.chips):
                    for c in range(2):
                        source = plan.hop(t, m) * sectors + 2 * q + c
                        moves.append((source, t * sectors + 2 * plan.spread[t][q] + c))
            own.append(lax.ppermute(right, ("term", "sector"), moves)[None])
        swapped = [lax.ppermute(x, "sector", cores) for x in own]
        return lefts, own, swapped
    everything = lax.all_gather(right, "sector").reshape((owners, groups, 2) + right.shape)
    by_chip = lax.dynamic_index_in_dim(everything, lax.axis_index("sector") % 2, 2, keepdims=False)
    spread_left = jnp.broadcast_to(left, (owners, 1) + left.shape)
    got = lax.all_to_all(jnp.concatenate([by_chip, spread_left], axis=1), "term", 0, 0)
    swapped = lax.ppermute(got[:, :groups], "sector", cores)
    lefts = [got[t, groups] for t in range(owners)]
    own = [got[t, :groups] for t in range(owners)]
    return lefts, own, [swapped[t] for t in range(owners)]


def local(plan, psi, left_env, right_env, precond, block_sizes):
    owners, sectors = plan.owners, plan.sectors
    devices = owners * sectors
    depth, width = right_env.shape[0], right_env.shape[-1]
    share = 2 * plan.groups
    lefts, own, swapped = inputs(plan, left_env[:, 0], right_env[:, 0])

    anywhere = pl.BlockSpec(memory_space=pltpu.HBM)
    vmem = pl.BlockSpec(memory_space=pltpu.VMEM)
    parked = [
        pltpu.with_memory_space_constraint(x, pltpu.HBM) for x in (block_sizes, psi[0], precond[0], lefts[0])
    ]
    terms, groups = owners * depth, plan.groups
    right_cat = pltpu.VMEM((terms * width, 2 * width), jnp.bfloat16)
    basis = jax.ShapeDtypeStruct((8, groups, width, width), jnp.float32)
    params = pltpu.CompilerParams(vmem_limit_bytes=32 << 20)
    flops = share * 7 * 3 * terms * width**3
    cost = pl.CostEstimate(flops=flops, bytes_accessed=1 << 20, transcendentals=0)
    *passed, own_basis = pl.pallas_call(
        functools.partial(own_kernel, plan),
        out_shape=(
            jax.ShapeDtypeStruct((width, terms * width), jnp.bfloat16),
            jax.ShapeDtypeStruct((groups, width, width), jnp.bfloat16),
            jax.ShapeDtypeStruct((groups, width, width), jnp.float32),
            jax.ShapeDtypeStruct((ROWS * 8, LANES), jnp.float32),
            basis,
        ),
        in_specs=[anywhere] * 4 + [vmem] * (2 * owners - 1),
        out_specs=(vmem,) * 5,
        scratch_shapes=[
            pltpu.SMEM((sectors,), jnp.int32),
            pltpu.VMEM((share, width, width), jnp.bfloat16),
            pltpu.VMEM((share, width, width), jnp.bfloat16),
            pltpu.VMEM((depth, width, width), jnp.bfloat16),
            right_cat,
            pltpu.SemaphoreType.DMA((4,)),
        ],
        compiler_params=params,
        cost_estimate=cost,
        name="own_columns",
    )(*parked, *lefts[1:], *own)
    gram, other_basis = pl.pallas_call(
        functools.partial(other_kernel, plan),
        out_shape=(jax.ShapeDtypeStruct((devices, LANES), jnp.float32), basis),
        in_specs=[vmem] * (4 + owners),
        out_specs=(vmem, vmem),
        scratch_shapes=[pltpu.VMEM((ROWS * 8, LANES), jnp.float32), right_cat],
        compiler_params=params,
        cost_estimate=cost,
        name="other_columns",
    )(*passed, *swapped)
    gram = lax.all_to_all(gram, ("term", "sector"), 0, 0, tiled=True)
    count = float(sectors * sectors * width * width)
    blocks, energy = pl.pallas_call(
        functools.partial(finish_kernel, count),
        out_shape=(
            jax.ShapeDtypeStruct((share, width, width), jnp.bfloat16),
            jax.ShapeDtypeStruct((1, LANES), jnp.float32),
        ),
        in_specs=[vmem] * 3,
        out_specs=(vmem, vmem),
        compiler_params=params,
        name="finish",
    )(gram, own_basis, other_basis)
    state = pl.pallas_call(
        functools.partial(assemble_kernel, plan),
        out_shape=jax.ShapeDtypeStruct((sectors, width, width), jnp.bfloat16),
        in_specs=[vmem] * owners,
        out_specs=anywhere,
        scratch_shapes=[pltpu.SemaphoreType.DMA((owners,))],
        compiler_params=pltpu.CompilerParams(vmem_limit_bytes=16 << 20),
        name="assemble",
    )(*[from_owner(plan, blocks, m) for m in range(owners)])
    return (state[None], energy[0, :3])


def solution(mesh):
    in_specs = (
        P("sector", None, None, None),
        P("term", "sector", None, None),
        P("term", "sector", None, None),
        P("sector", None, None, None),
        P(),
    )
    out_specs = (P("sector", None, None, None), P())
    return jax.shard_map(
        functools.partial(local, Plan(mesh.shape["term"], mesh.shape["sector"])),
        mesh=mesh,
        in_specs=in_specs,
        out_specs=out_specs,
        check_vma=False,
    )
```

```python
import functools

import jax
import jax.numpy as jnp
from jax import lax
from jax.experimental import pallas as pl
from jax.experimental.pallas import tpu as pltpu
from jax.sharding import PartitionSpec as P

EPS = 1e-06
SCALE = 2.0**-12
UNSCALE = 2.0**12
ROWS = 64
LANES = 128

POWERS = ((0, 0), (0, 1), (1, 0), (1, 1))
N0, E0 = 0, 1
N1, E1 = 2, 5
N2, E2 = 8, 17
N3 = 26


def split(x):
    high = x.astype(jnp.bfloat16)
    low = (x - high.astype(jnp.float32)).astype(jnp.bfloat16)
    return jnp.concatenate([high, low], axis=1)


def fold(x):
    return functools.reduce(lambda a, b: a + b, [x[r : r + 8] for r in range(0, x.shape[0], 8)])


def stack_right(plan, right_cat, right_refs, g, width):
    depth = right_refs[0].shape[1]
    for k in range(plan.owners * depth):
        rows, ref = slice(k * width, (k + 1) * width), right_refs[plan.places[k // depth]]
        for half in range(2):
            right_cat[rows, half * width : (half + 1) * width] = ref[g, k % depth]


def levels(left_cat, right_cats, sums, basis_ref, slots, starts, inverses):
    width = starts[0].shape[0]
    terms = left_cat.shape[1] // width
    some = range(len(starts))

    def apply(vectors):
        columns = []
        for b in some:
            stacked = jnp.concatenate(vectors[b], axis=0)
            images = lax.dot_general(
                stacked,
                right_cats[b][:, : stacked.shape[1]],
                (((1,), (1,)), ((), ())),
                preferred_element_type=jnp.float32,
            ).astype(jnp.bfloat16)
            for n in range(len(vectors[b])):
                rows = images[n * width : (n + 1) * width]
                columns.append(jnp.concatenate([rows[:, k * width : (k + 1) * width] for k in range(terms)], axis=0))
        out = jnp.dot(left_cat[...], jnp.concatenate(columns, axis=1), preferred_element_type=jnp.float32)
        count = len(vectors[0])
        return [[out[:, (b * count + n) * width : (b * count + n + 1) * width] for n in range(count)] for b in some]

    def add(slot, value):
        sums[slot * 8 : slot * 8 + 8] += value

    def put(table, at, value):
        table[at] = value if table[at] is None else table[at] + value

    def advance(vectors, images):
        level = []
        for b in some:
            level.append([])
            for x, h in zip(vectors[b], images[b]):
                level[b] += [SCALE * x - (SCALE * inverses[b]) * h, inverses[b] * x]
        return level

    images = apply([[start] for start in starts])
    zeroth = [[start.astype(jnp.float32)] for start in starts]
    for b in some:
        add(N0, fold(zeroth[b][0] * zeroth[b][0]))
        add(E0, fold(zeroth[b][0] * images[b][0]))
    first = advance(zeroth, images)

    images = apply([[split(x) for x in vectors] for vectors in first])
    for b in some:
        for m in range(2):
            for n in range(2):
                if m <= n:
                    add(N1 + m + n, (1.0 if m == n else 2.0) * fold(first[b][m] * first[b][n]))
                add(E1 + m + n, fold(first[b][m] * images[b][n]))
    second = advance(first, images)

    images = apply([[split(x) for x in vectors] for vectors in second])
    third = advance(second, images)
    for b in some:
        for m in range(8):
            basis_ref[m, slots[b]] = third[b][m]
        norm, energy, last = [None] * 9, [None] * 9, [None] * 27
        for m in range(4):
            for n in range(4):
                a0, a1 = POWERS[m][0] + POWERS[n][0], POWERS[m][1] + POWERS[n][1]
                put(energy, 3 * a0 + a1, fold(second[b][m] * images[b][n]))
                if m <= n:
                    put(norm, 3 * a0 + a1, (1.0 if m == n else 2.0) * fold(second[b][m] * second[b][n]))
                for d in range(2):
                    for e in range(2):
                        if (m, d) <= (n, e):
                            scale = 1.0 if (m, d) == (n, e) else 2.0
                            put(last, 9 * a0 + 3 * a1 + d + e, scale * fold(third[b][2 * m + d] * third[b][2 * n + e]))
        for at in range(9):
            add(N2 + at, norm[at])
            add(E2 + at, energy[at])
        for at in range(27):
            add(N3 + at, last[at])


def each_group(groups, body):
    if groups == 1:
        body(0)
    else:
        pl.loop(0, groups)(body)


def prepare_kernel(plan, sizes_hbm, psi_hbm, pre_hbm, *refs):
    own_refs, refs = refs[: plan.owners], refs[plan.owners :]
    own_cat, start_ref, inverse_ref, sizes_ref, psi_ref, pre_ref, sems = refs
    width = psi_ref.shape[-1]
    row = lax.axis_index("sector")
    core = row % 2
    chip = plan.first_chip(lax.axis_index("term"), row // 2)
    blocks = pl.ds(2 * chip, psi_ref.shape[0])
    copies = [
        pltpu.make_async_copy(sizes_hbm, sizes_ref, sems.at[0]),
        pltpu.make_async_copy(psi_hbm.at[blocks], psi_ref, sems.at[1]),
        pltpu.make_async_copy(pre_hbm.at[blocks], pre_ref, sems.at[2]),
    ]
    for copy in copies:
        copy.start()
    each_group(plan.groups, lambda g: stack_right(plan, own_cat.at[g], own_refs, g, psi_ref.shape[-1]))
    for copy in copies:
        copy.wait()
    row_ids = lax.broadcasted_iota(jnp.int32, (width, width), 0)
    col_ids = lax.broadcasted_iota(jnp.int32, (width, width), 1)

    def body(g):
        for b in range(2):
            block = 2 * g + (core if b == 0 else 1 - core)
            valid = (row_ids < sizes_ref[row]) & (col_ids < sizes_ref[2 * chip + block])
            start_ref[b, g] = jnp.where(valid, psi_ref[block].astype(jnp.float32), 0.0).astype(jnp.bfloat16)
            inverse_ref[b, g] = jnp.where(valid, 1.0 / pre_ref[block].astype(jnp.float32), 0.0)

    each_group(plan.groups, body)


def levels_kernel(plan, pieces, own_cat, start_ref, inverse_ref, *refs):
    left_refs, swap_refs, refs = refs[:pieces], refs[pieces : pieces + plan.owners], refs[pieces + plan.owners :]
    gram_ref, basis_ref, left_cat, swap_cat, sums = refs
    width = left_cat.shape[0]
    sums[...] = jnp.zeros_like(sums)
    for k, (ref, at) in enumerate((ref, at) for ref in left_refs for at in range(ref.shape[0])):
        left_cat[:, k * width : (k + 1) * width] = ref[at]

    def body(g):
        stack_right(plan, swap_cat, swap_refs, g, width)
        starts = [start_ref[b, g] for b in range(2)]
        inverses = [inverse_ref[b, g] for b in range(2)]
        levels(left_cat, (own_cat.at[g], swap_cat), sums, basis_ref, (2 * g, 2 * g + 1), starts, inverses)

    each_group(plan.groups, body)
    folded = functools.reduce(lambda a, b: a + b, [sums[pl.ds(s, ROWS, stride=8), :] for s in range(8)])
    totals = jnp.sum(folded, axis=1, keepdims=True)
    row_ids = lax.broadcasted_iota(jnp.int32, (ROWS, LANES), 0)
    col_ids = lax.broadcasted_iota(jnp.int32, (ROWS, LANES), 1)
    line = jnp.sum(jnp.where(row_ids == col_ids, totals, 0.0), axis=0, keepdims=True)
    gram_ref[...] = jnp.broadcast_to(line, gram_ref.shape)


def finish_kernel(count, gram_ref, basis_ref, out_ref, energy_ref):
    core = lax.axis_index("sector") % 2
    share = out_ref.shape[0]
    gram = jnp.sum(gram_ref[...], axis=0, keepdims=True)
    lane = lax.broadcasted_iota(jnp.int32, (1, LANES), 1)

    def total(base, size, weight):
        inside = (lane >= base) & (lane < base + size)
        return jnp.sum(jnp.where(inside, gram * weight, 0.0), axis=1, keepdims=True)

    def power(exponent, value):
        return jnp.where(exponent == 0, 1.0, jnp.where(exponent == 1, value, value * value))

    theta0 = total(E0, 1, 1.0) / total(N0, 1, 1.0)
    tau0 = SCALE * theta0
    norm1 = total(N1, 3, power(lane - N1, tau0))
    theta1 = total(E1, 3, power(lane - E1, tau0)) / norm1
    tau1 = SCALE * theta1

    def weight2(base):
        at = lane - base
        return power(at // 3, tau0) * power(at % 3, tau1)

    norm2 = total(N2, 9, weight2(N2))
    theta2 = total(E2, 9, weight2(E2)) / norm2
    tau2 = SCALE * theta2
    at = lane - N3
    norm3 = total(N3, 27, power(at // 9, tau0) * power(at // 3 % 3, tau1) * power(at % 3, tau2))

    def factor(gain, norm):
        return lax.rsqrt(gain * gain * jnp.maximum(norm, 0.0) / count + EPS)

    gain = jnp.full((1, 1), UNSCALE, jnp.float32)
    gain = factor(gain, norm1) * gain * UNSCALE
    gain = factor(gain, norm2) * gain * UNSCALE
    gain = factor(gain, norm3) * gain
    weights = [gain, gain * tau1, gain * tau0, gain * tau0 * tau1]
    for at in range(share):
        even = at % 2 == 0
        value = None
        for m in range(4):
            part = weights[m] * (basis_ref[2 * m, at] + tau2 * basis_ref[2 * m + 1, at])
            value = part if value is None else value + part
        block = (at // 2) * 2 + (core if even else 1 - core)
        out_ref[block] = value.astype(jnp.bfloat16)
    energy_ref[...] = jnp.where(lane == 0, theta0, jnp.where(lane == 1, theta1, theta2))


def assemble_kernel(plan, *refs):
    pieces, out_ref, sems = refs[: plan.owners], refs[plan.owners], refs[plan.owners + 1]
    share = pieces[0].shape[0]
    term, chip = lax.axis_index("term"), lax.axis_index("sector") // 2
    copies = []
    for m in range(plan.owners):
        first = plan.first_chip(plan.hop(term, m), chip) * 2
        copies.append(pltpu.make_async_copy(pieces[m], out_ref.at[pl.ds(first, share)], sems.at[m]))
        copies[-1].start()
    for copy in copies:
        copy.wait()


class Plan:
    def __init__(self, owners, sectors):
        self.owners, self.sectors, self.chips = owners, sectors, sectors // 2
        self.groups = self.chips // owners
        self.direct = self.groups == 1 and owners > 1 and owners & (owners - 1) == 0
        self.bits = [1 << b for b in reversed(range(owners.bit_length() - 1))]
        self.order = (0, 3, 1, 2) if self.direct and owners == 4 else tuple(range(owners))
        offsets = [0]
        for bit in self.bits if self.direct else []:
            offsets = offsets + [offset ^ bit for offset in offsets]
        self.places = [self.order.index(offset) for offset in offsets] if self.direct else self.order
        if owners == 4:
            self.spread = ((0, 2, 1, 3), (1, 3, 0, 2), (2, 0, 3, 1), (3, 1, 2, 0))
        else:
            self.spread = tuple(tuple((q + t) % owners for q in range(owners)) for t in range(owners))

    def hop(self, term, offset):
        if self.owners & (self.owners - 1) == 0:
            return term ^ offset
        return (term + offset) % self.owners

    def back(self, offset):
        if self.owners & (self.owners - 1) == 0:
            return offset
        return (self.owners - offset) % self.owners

    def first_chip(self, term, chip):
        if not self.direct:
            return term * self.groups
        found = jnp.int32(0)
        for t in range(self.owners):
            for q in range(self.owners):
                hit = (term == t) & (chip == self.spread[t][q])
                found = jnp.where(hit, q, found)
        return found


def from_owner(plan, value, offset):
    if offset == 0:
        return value
    moves = [(plan.hop(t, offset), t) for t in range(plan.owners)]
    return lax.ppermute(value, "term", moves)


def inputs(plan, left, right):
    sectors, owners, groups = plan.sectors, plan.owners, plan.groups
    cores = [(i, i ^ 1) for i in range(sectors)]
    if plan.direct:
        held = left
        for bit in plan.bits:
            lefts = [held, from_owner(plan, held, bit)]
            held = jnp.concatenate(lefts, axis=0)
        own = {}
        for m in plan.order:
            moves = []
            for t in range(owners):
                for q in range(plan.chips):
                    for c in range(2):
                        source = plan.hop(t, m) * sectors + 2 * q + c
                        moves.append((source, t * sectors + 2 * plan.spread[t][q] + c))
            own[m] = lax.ppermute(right, ("term", "sector"), moves)[None]
        own = [own[m] for m in plan.order]
        swapped = [lax.ppermute(x, "sector", cores) for x in own]
        return lefts, own, swapped
    everything = lax.all_gather(right, "sector").reshape((owners, groups, 2) + right.shape)
    by_chip = lax.dynamic_index_in_dim(everything, lax.axis_index("sector") % 2, 2, keepdims=False)
    spread_left = jnp.broadcast_to(left, (owners, 1) + left.shape)
    got = lax.all_to_all(jnp.concatenate([by_chip, spread_left], axis=1), "term", 0, 0)
    swapped = lax.ppermute(got[:, :groups], "sector", cores)
    lefts = [got[t, groups] for t in range(owners)]
    own = [got[t, :groups] for t in range(owners)]
    return lefts, own, [swapped[t] for t in range(owners)]


def local(plan, psi, left_env, right_env, precond, block_sizes):
    owners, sectors = plan.owners, plan.sectors
    devices = owners * sectors
    depth, width = right_env.shape[0], right_env.shape[-1]
    share = 2 * plan.groups
    lefts, own, swapped = inputs(plan, left_env[:, 0], right_env[:, 0])
    pieces = len(lefts)

    anywhere = pl.BlockSpec(memory_space=pltpu.HBM)
    vmem = pl.BlockSpec(memory_space=pltpu.VMEM)
    parked = [pltpu.with_memory_space_constraint(x, pltpu.HBM) for x in (block_sizes, psi[0], precond[0])]
    terms, groups = owners * depth, plan.groups
    params = pltpu.CompilerParams(vmem_limit_bytes=32 << 20)
    prepared = pl.pallas_call(
        functools.partial(prepare_kernel, plan),
        out_shape=(
            jax.ShapeDtypeStruct((groups, terms * width, 2 * width), jnp.bfloat16),
            jax.ShapeDtypeStruct((2, groups, width, width), jnp.bfloat16),
            jax.ShapeDtypeStruct((2, groups, width, width), jnp.float32),
        ),
        in_specs=[anywhere] * 3 + [vmem] * owners,
        out_specs=(vmem,) * 3,
        scratch_shapes=[
            pltpu.SMEM((sectors,), jnp.int32),
            pltpu.VMEM((share, width, width), jnp.bfloat16),
            pltpu.VMEM((share, width, width), jnp.bfloat16),
            pltpu.SemaphoreType.DMA((3,)),
        ],
        compiler_params=params,
        name="prepare",
    )(*parked, *own)
    gram, basis = pl.pallas_call(
        functools.partial(levels_kernel, plan, pieces),
        out_shape=(
            jax.ShapeDtypeStruct((devices, LANES), jnp.float32),
            jax.ShapeDtypeStruct((8, share, width, width), jnp.float32),
        ),
        in_specs=[vmem] * (3 + pieces + owners),
        out_specs=(vmem, vmem),
        scratch_shapes=[
            pltpu.VMEM((width, terms * width), jnp.bfloat16),
            pltpu.VMEM((terms * width, 2 * width), jnp.bfloat16),
            pltpu.VMEM((ROWS * 8, LANES), jnp.float32),
        ],
        compiler_params=params,
        name="levels",
    )(*prepared, *lefts, *swapped)
    gram = lax.all_to_all(gram, ("term", "sector"), 0, 0, tiled=True)
    count = float(sectors * sectors * width * width)
    blocks, energy = pl.pallas_call(
        functools.partial(finish_kernel, count),
        out_shape=(
            jax.ShapeDtypeStruct((share, width, width), jnp.bfloat16),
            jax.ShapeDtypeStruct((1, LANES), jnp.float32),
        ),
        in_specs=[vmem, vmem],
        out_specs=(vmem, vmem),
        compiler_params=params,
        name="finish",
    )(gram, basis)
    state = pl.pallas_call(
        functools.partial(assemble_kernel, plan),
        out_shape=jax.ShapeDtypeStruct((sectors, width, width), jnp.bfloat16),
        in_specs=[vmem] * owners,
        out_specs=anywhere,
        scratch_shapes=[pltpu.SemaphoreType.DMA((owners,))],
        compiler_params=pltpu.CompilerParams(vmem_limit_bytes=16 << 20),
        name="assemble",
    )(*[from_owner(plan, blocks, m) for m in range(owners)])
    return (state[None], energy[0, :3])


def solution(mesh):
    in_specs = (
        P("sector", None, None, None),
        P("term", "sector", None, None),
        P("term", "sector", None, None),
        P("sector", None, None, None),
        P(),
    )
    out_specs = (P("sector", None, None, None), P())
    return jax.shard_map(
        functools.partial(local, Plan(mesh.shape["term"], mesh.shape["sector"])),
        mesh=mesh,
        in_specs=in_specs,
        out_specs=out_specs,
        check_vma=False,
    )
```

```python
import functools

import jax
import jax.numpy as jnp
from jax import lax
from jax.experimental import pallas as pl
from jax.experimental.pallas import tpu as pltpu
from jax.sharding import PartitionSpec as P

EPS = 1e-06
SCALE = 2.0**-12
UNSCALE = 2.0**12
ROWS = 64
LANES = 128

POWERS = ((0, 0), (0, 1), (1, 0), (1, 1))
N0, E0 = 0, 1
N1, E1 = 2, 5
N2, E2 = 8, 17
N3 = 26


def split(x):
    high = x.astype(jnp.bfloat16)
    low = (x - high.astype(jnp.float32)).astype(jnp.bfloat16)
    return jnp.concatenate([high, low], axis=1)


def fold(x):
    return functools.reduce(lambda a, b: a + b, [x[r : r + 8] for r in range(0, x.shape[0], 8)])


def stack_right(plan, right_cat, right_refs, g, width):
    depth = right_refs[0].shape[1]
    for k in range(plan.owners * depth):
        rows, ref = slice(k * width, (k + 1) * width), right_refs[plan.places[k // depth]]
        for half in range(2):
            right_cat[rows, half * width : (half + 1) * width] = ref[g, k % depth]


def levels(left_cat, right_cats, sums, basis_ref, slots, starts, inverses):
    width = starts[0].shape[0]
    terms = left_cat.shape[1] // width
    some = range(len(starts))

    def apply(vectors):
        columns = []
        for b in some:
            stacked = jnp.concatenate(vectors[b], axis=0)
            images = lax.dot_general(
                stacked,
                right_cats[b][:, : stacked.shape[1]],
                (((1,), (1,)), ((), ())),
                preferred_element_type=jnp.float32,
            ).astype(jnp.bfloat16)
            for n in range(len(vectors[b])):
                rows = images[n * width : (n + 1) * width]
                columns.append(jnp.concatenate([rows[:, k * width : (k + 1) * width] for k in range(terms)], axis=0))
        out = jnp.dot(left_cat[...], jnp.concatenate(columns, axis=1), preferred_element_type=jnp.float32)
        count = len(vectors[0])
        return [[out[:, (b * count + n) * width : (b * count + n + 1) * width] for n in range(count)] for b in some]

    def add(slot, value):
        sums[slot * 8 : slot * 8 + 8] += value

    def put(table, at, value):
        table[at] = value if table[at] is None else table[at] + value

    def advance(vectors, images):
        level = []
        for b in some:
            level.append([])
            for x, h in zip(vectors[b], images[b]):
                level[b] += [SCALE * x - (SCALE * inverses[b]) * h, inverses[b] * x]
        return level

    images = apply([[start] for start in starts])
    zeroth = [[start.astype(jnp.float32)] for start in starts]
    for b in some:
        add(N0, fold(zeroth[b][0] * zeroth[b][0]))
        add(E0, fold(zeroth[b][0] * images[b][0]))
    first = advance(zeroth, images)

    images = apply([[split(x) for x in vectors] for vectors in first])
    for b in some:
        for m in range(2):
            for n in range(2):
                if m <= n:
                    add(N1 + m + n, (1.0 if m == n else 2.0) * fold(first[b][m] * first[b][n]))
                add(E1 + m + n, fold(first[b][m] * images[b][n]))
    second = advance(first, images)

    images = apply([[split(x) for x in vectors] for vectors in second])
    third = advance(second, images)
    for b in some:
        for m in range(8):
            basis_ref[m, slots[b]] = third[b][m]
        norm, energy, last = [None] * 9, [None] * 9, [None] * 27
        for m in range(4):
            for n in range(4):
                a0, a1 = POWERS[m][0] + POWERS[n][0], POWERS[m][1] + POWERS[n][1]
                put(energy, 3 * a0 + a1, fold(second[b][m] * images[b][n]))
                if m <= n:
                    put(norm, 3 * a0 + a1, (1.0 if m == n else 2.0) * fold(second[b][m] * second[b][n]))
                for d in range(2):
                    for e in range(2):
                        if (m, d) <= (n, e):
                            scale = 1.0 if (m, d) == (n, e) else 2.0
                            put(last, 9 * a0 + 3 * a1 + d + e, scale * fold(third[b][2 * m + d] * third[b][2 * n + e]))
        for at in range(9):
            add(N2 + at, norm[at])
            add(E2 + at, energy[at])
        for at in range(27):
            add(N3 + at, last[at])


def each_group(groups, body):
    if groups == 1:
        body(0)
    else:
        pl.loop(0, groups)(body)


def prepare_kernel(plan, sizes_hbm, psi_hbm, pre_hbm, *refs):
    own_refs, refs = refs[: plan.owners], refs[plan.owners :]
    own_cat, start_ref, inverse_ref, sizes_ref, psi_ref, pre_ref, sems = refs
    width = psi_ref.shape[-1]
    row = lax.axis_index("sector")
    core = row % 2
    chip = plan.first_chip(lax.axis_index("term"), row // 2)
    blocks = pl.ds(2 * chip, psi_ref.shape[0])
    copies = [
        pltpu.make_async_copy(sizes_hbm, sizes_ref, sems.at[0]),
        pltpu.make_async_copy(psi_hbm.at[blocks], psi_ref, sems.at[1]),
        pltpu.make_async_copy(pre_hbm.at[blocks], pre_ref, sems.at[2]),
    ]
    for copy in copies:
        copy.start()
    each_group(plan.groups, lambda g: stack_right(plan, own_cat.at[g], own_refs, g, psi_ref.shape[-1]))
    for copy in copies:
        copy.wait()
    row_ids = lax.broadcasted_iota(jnp.int32, (width, width), 0)
    col_ids = lax.broadcasted_iota(jnp.int32, (width, width), 1)

    def body(g):
        for b in range(2):
            block = 2 * g + (core if b == 0 else 1 - core)
            valid = (row_ids < sizes_ref[row]) & (col_ids < sizes_ref[2 * chip + block])
            start_ref[b, g] = jnp.where(valid, psi_ref[block].astype(jnp.float32), 0.0).astype(jnp.bfloat16)
            inverse_ref[b, g] = jnp.where(valid, 1.0 / pre_ref[block].astype(jnp.float32), 0.0)

    each_group(plan.groups, body)


def join_kernel(own_hbm, *refs):
    held_refs, out_ref, sem = refs[:-2], refs[-2], refs[-1]
    base = own_hbm.shape[0]
    copy = pltpu.make_async_copy(own_hbm, out_ref.at[:base], sem)
    copy.start()
    for ref in held_refs:
        out_ref[base : base + ref.shape[0]] = ref[...]
        base += ref.shape[0]
    copy.wait()


def join(own, *held):
    rows = own.shape[0] + sum(x.shape[0] for x in held)
    vmem = pl.BlockSpec(memory_space=pltpu.VMEM)
    return pl.pallas_call(
        join_kernel,
        out_shape=jax.ShapeDtypeStruct((rows,) + own.shape[1:], own.dtype),
        in_specs=[pl.BlockSpec(memory_space=pltpu.HBM)] + [vmem] * len(held),
        out_specs=vmem,
        scratch_shapes=[pltpu.SemaphoreType.DMA],
        compiler_params=pltpu.CompilerParams(vmem_limit_bytes=16 << 20),
        name="join",
    )(pltpu.with_memory_space_constraint(own, pltpu.HBM), *held)


def levels_kernel(plan, pieces, own_cat, start_ref, inverse_ref, *refs):
    left_refs, swap_refs, refs = refs[:pieces], refs[pieces : pieces + plan.owners], refs[pieces + plan.owners :]
    gram_ref, basis_ref, left_cat, swap_cat, sums = refs
    width = left_cat.shape[0]
    sums[...] = jnp.zeros_like(sums)
    for k, (ref, at) in enumerate((ref, at) for ref in left_refs for at in range(ref.shape[0])):
        left_cat[:, k * width : (k + 1) * width] = ref[at]

    def body(g):
        stack_right(plan, swap_cat, swap_refs, g, width)
        starts = [start_ref[b, g] for b in range(2)]
        inverses = [inverse_ref[b, g] for b in range(2)]
        levels(left_cat, (own_cat.at[g], swap_cat), sums, basis_ref, (2 * g, 2 * g + 1), starts, inverses)

    each_group(plan.groups, body)
    folded = functools.reduce(lambda a, b: a + b, [sums[pl.ds(s, ROWS, stride=8), :] for s in range(8)])
    totals = jnp.sum(folded, axis=1, keepdims=True)
    row_ids = lax.broadcasted_iota(jnp.int32, (ROWS, LANES), 0)
    col_ids = lax.broadcasted_iota(jnp.int32, (ROWS, LANES), 1)
    line = jnp.sum(jnp.where(row_ids == col_ids, totals, 0.0), axis=0, keepdims=True)
    gram_ref[...] = jnp.broadcast_to(line, gram_ref.shape)


def finish_kernel(count, gram_ref, basis_ref, out_ref, energy_ref):
    core = lax.axis_index("sector") % 2
    share = out_ref.shape[0]
    gram = jnp.sum(gram_ref[...], axis=0, keepdims=True)
    lane = lax.broadcasted_iota(jnp.int32, (1, LANES), 1)

    def total(base, size, weight):
        inside = (lane >= base) & (lane < base + size)
        return jnp.sum(jnp.where(inside, gram * weight, 0.0), axis=1, keepdims=True)

    def power(exponent, value):
        return jnp.where(exponent == 0, 1.0, jnp.where(exponent == 1, value, value * value))

    theta0 = total(E0, 1, 1.0) / total(N0, 1, 1.0)
    tau0 = SCALE * theta0
    norm1 = total(N1, 3, power(lane - N1, tau0))
    theta1 = total(E1, 3, power(lane - E1, tau0)) / norm1
    tau1 = SCALE * theta1

    def weight2(base):
        at = lane - base
        return power(at // 3, tau0) * power(at % 3, tau1)

    norm2 = total(N2, 9, weight2(N2))
    theta2 = total(E2, 9, weight2(E2)) / norm2
    tau2 = SCALE * theta2
    at = lane - N3
    norm3 = total(N3, 27, power(at // 9, tau0) * power(at // 3 % 3, tau1) * power(at % 3, tau2))

    def factor(gain, norm):
        return lax.rsqrt(gain * gain * jnp.maximum(norm, 0.0) / count + EPS)

    gain = jnp.full((1, 1), UNSCALE, jnp.float32)
    gain = factor(gain, norm1) * gain * UNSCALE
    gain = factor(gain, norm2) * gain * UNSCALE
    gain = factor(gain, norm3) * gain
    weights = [gain, gain * tau1, gain * tau0, gain * tau0 * tau1]
    for at in range(share):
        even = at % 2 == 0
        value = None
        for m in range(4):
            part = weights[m] * (basis_ref[2 * m, at] + tau2 * basis_ref[2 * m + 1, at])
            value = part if value is None else value + part
        block = (at // 2) * 2 + (core if even else 1 - core)
        out_ref[block] = value.astype(jnp.bfloat16)
    energy_ref[...] = jnp.where(lane == 0, theta0, jnp.where(lane == 1, theta1, theta2))


def assemble_kernel(plan, *refs):
    pieces, out_ref, sems = refs[: plan.owners], refs[plan.owners], refs[plan.owners + 1]
    share = pieces[0].shape[0]
    term, chip = lax.axis_index("term"), lax.axis_index("sector") // 2
    copies = []
    for m in range(plan.owners):
        first = plan.first_chip(plan.hop(term, m), chip) * 2
        copies.append(pltpu.make_async_copy(pieces[m], out_ref.at[pl.ds(first, share)], sems.at[m]))
        copies[-1].start()
    for copy in copies:
        copy.wait()


class Plan:
    def __init__(self, owners, sectors):
        self.owners, self.sectors, self.chips = owners, sectors, sectors // 2
        self.groups = self.chips // owners
        self.direct = self.groups == 1 and owners > 1 and owners & (owners - 1) == 0
        self.bits = [1 << b for b in reversed(range(owners.bit_length() - 1))]
        self.order = (0, 2, 3, 1) if self.direct and owners == 4 else tuple(range(owners))
        offsets = [0]
        for bit in self.bits if self.direct else []:
            offsets = offsets + [offset ^ bit for offset in offsets]
        self.places = [self.order.index(offset) for offset in offsets] if self.direct else self.order
        if owners == 4:
            self.spread = ((1, 0, 3, 2), (0, 2, 1, 3), (2, 3, 0, 1), (3, 1, 2, 0))
        else:
            self.spread = tuple(tuple((q + t) % owners for q in range(owners)) for t in range(owners))

    def hop(self, term, offset):
        if self.owners & (self.owners - 1) == 0:
            return term ^ offset
        return (term + offset) % self.owners

    def back(self, offset):
        if self.owners & (self.owners - 1) == 0:
            return offset
        return (self.owners - offset) % self.owners

    def first_chip(self, term, chip):
        if not self.direct:
            return term * self.groups
        found = jnp.int32(0)
        for t in range(self.owners):
            for q in range(self.owners):
                hit = (term == t) & (chip == self.spread[t][q])
                found = jnp.where(hit, q, found)
        return found


def from_owner(plan, value, offset):
    if offset == 0:
        return value
    moves = [(plan.hop(t, offset), t) for t in range(plan.owners)]
    return lax.ppermute(value, "term", moves)


def inputs(plan, left, right):
    sectors, owners, groups = plan.sectors, plan.owners, plan.groups
    cores = [(i, i ^ 1) for i in range(sectors)]
    if plan.direct:
        lefts, held = [left], []
        for bit in plan.bits:
            lefts = [join(left, *held) if held else left]
            held.append(from_owner(plan, lefts[0], bit))
        lefts.append(held[-1])
        own = {}
        for m in plan.order:
            moves = []
            for t in range(owners):
                for q in range(plan.chips):
                    for c in range(2):
                        source = plan.hop(t, m) * sectors + 2 * q + c
                        moves.append((source, t * sectors + 2 * plan.spread[t][q] + c))
            own[m] = lax.ppermute(right, ("term", "sector"), moves)[None]
        own = [own[m] for m in plan.order]
        swapped = [lax.ppermute(x, "sector", cores) for x in own]
        return lefts, own, swapped
    everything = lax.all_gather(right, "sector").reshape((owners, groups, 2) + right.shape)
    by_chip = lax.dynamic_index_in_dim(everything, lax.axis_index("sector") % 2, 2, keepdims=False)
    spread_left = jnp.broadcast_to(left, (owners, 1) + left.shape)
    got = lax.all_to_all(jnp.concatenate([by_chip, spread_left], axis=1), "term", 0, 0)
    swapped = lax.ppermute(got[:, :groups], "sector", cores)
    lefts = [got[t, groups] for t in range(owners)]
    own = [got[t, :groups] for t in range(owners)]
    return lefts, own, [swapped[t] for t in range(owners)]


def local(plan, psi, left_env, right_env, precond, block_sizes):
    owners, sectors = plan.owners, plan.sectors
    devices = owners * sectors
    depth, width = right_env.shape[0], right_env.shape[-1]
    share = 2 * plan.groups
    lefts, own, swapped = inputs(plan, left_env[:, 0], right_env[:, 0])
    pieces = len(lefts)

    anywhere = pl.BlockSpec(memory_space=pltpu.HBM)
    vmem = pl.BlockSpec(memory_space=pltpu.VMEM)
    parked = [pltpu.with_memory_space_constraint(x, pltpu.HBM) for x in (block_sizes, psi[0], precond[0])]
    terms, groups = owners * depth, plan.groups
    params = pltpu.CompilerParams(vmem_limit_bytes=32 << 20)
    prepared = pl.pallas_call(
        functools.partial(prepare_kernel, plan),
        out_shape=(
            jax.ShapeDtypeStruct((groups, terms * width, 2 * width), jnp.bfloat16),
            jax.ShapeDtypeStruct((2, groups, width, width), jnp.bfloat16),
            jax.ShapeDtypeStruct((2, groups, width, width), jnp.float32),
        ),
        in_specs=[anywhere] * 3 + [vmem] * owners,
        out_specs=(vmem,) * 3,
        scratch_shapes=[
            pltpu.SMEM((sectors,), jnp.int32),
            pltpu.VMEM((share, width, width), jnp.bfloat16),
            pltpu.VMEM((share, width, width), jnp.bfloat16),
            pltpu.SemaphoreType.DMA((3,)),
        ],
        compiler_params=params,
        name="prepare",
    )(*parked, *own)
    gram, basis = pl.pallas_call(
        functools.partial(levels_kernel, plan, pieces),
        out_shape=(
            jax.ShapeDtypeStruct((devices, LANES), jnp.float32),
            jax.ShapeDtypeStruct((8, share, width, width), jnp.float32),
        ),
        in_specs=[vmem] * (3 + pieces + owners),
        out_specs=(vmem, vmem),
        scratch_shapes=[
            pltpu.VMEM((width, terms * width), jnp.bfloat16),
            pltpu.VMEM((terms * width, 2 * width), jnp.bfloat16),
            pltpu.VMEM((ROWS * 8, LANES), jnp.float32),
        ],
        compiler_params=params,
        name="levels",
    )(*prepared, *lefts, *swapped)
    gram = lax.all_to_all(gram, ("term", "sector"), 0, 0, tiled=True)
    count = float(sectors * sectors * width * width)
    blocks, energy = pl.pallas_call(
        functools.partial(finish_kernel, count),
        out_shape=(
            jax.ShapeDtypeStruct((share, width, width), jnp.bfloat16),
            jax.ShapeDtypeStruct((1, LANES), jnp.float32),
        ),
        in_specs=[vmem, vmem],
        out_specs=(vmem, vmem),
        compiler_params=params,
        name="finish",
    )(gram, basis)
    state = pl.pallas_call(
        functools.partial(assemble_kernel, plan),
        out_shape=jax.ShapeDtypeStruct((sectors, width, width), jnp.bfloat16),
        in_specs=[vmem] * owners,
        out_specs=anywhere,
        scratch_shapes=[pltpu.SemaphoreType.DMA((owners,))],
        compiler_params=pltpu.CompilerParams(vmem_limit_bytes=16 << 20),
        name="assemble",
    )(*[from_owner(plan, blocks, m) for m in range(owners)])
    return (state[None], energy[0, :3])


def solution(mesh):
    in_specs = (
        P("sector", None, None, None),
        P("term", "sector", None, None),
        P("term", "sector", None, None),
        P("sector", None, None, None),
        P(),
    )
    out_specs = (P("sector", None, None, None), P())
    return jax.shard_map(
        functools.partial(local, Plan(mesh.shape["term"], mesh.shape["sector"])),
        mesh=mesh,
        in_specs=in_specs,
        out_specs=out_specs,
        check_vma=False,
    )
```

```python
import functools

import jax
import jax.numpy as jnp
from jax import lax
from jax.experimental import pallas as pl
from jax.experimental.pallas import tpu as pltpu
from jax.sharding import PartitionSpec as P

EPS = 1e-06
SCALE = 2.0**-12
UNSCALE = 2.0**12
ROWS = 64
LANES = 128

POWERS = ((0, 0), (0, 1), (1, 0), (1, 1))
N0, E0 = 0, 1
N1, E1 = 2, 5
N2, E2 = 8, 17
N3 = 26


def split(x):
    high = x.astype(jnp.bfloat16)
    low = (x - high.astype(jnp.float32)).astype(jnp.bfloat16)
    return jnp.concatenate([high, low], axis=1)


def fold(x):
    return functools.reduce(lambda a, b: a + b, [x[r : r + 8] for r in range(0, x.shape[0], 8)])


def stack_right(plan, right_cat, right_refs, g, width):
    depth = right_refs[0].shape[1]
    for k in range(plan.owners * depth):
        rows, ref = slice(k * width, (k + 1) * width), right_refs[plan.places[k // depth]]
        for half in range(2):
            right_cat[rows, half * width : (half + 1) * width] = ref[g, k % depth]


def levels(left_cat, right_cats, sums, basis_ref, slots, starts, inverses):
    width = starts[0].shape[0]
    terms = left_cat.shape[1] // width
    some = range(len(starts))

    def apply(vectors):
        columns = []
        for b in some:
            stacked = jnp.concatenate(vectors[b], axis=0)
            images = lax.dot_general(
                stacked,
                right_cats[b][:, : stacked.shape[1]],
                (((1,), (1,)), ((), ())),
                preferred_element_type=jnp.float32,
            ).astype(jnp.bfloat16)
            for n in range(len(vectors[b])):
                rows = images[n * width : (n + 1) * width]
                columns.append(jnp.concatenate([rows[:, k * width : (k + 1) * width] for k in range(terms)], axis=0))
        out = jnp.dot(left_cat[...], jnp.concatenate(columns, axis=1), preferred_element_type=jnp.float32)
        count = len(vectors[0])
        return [[out[:, (b * count + n) * width : (b * count + n + 1) * width] for n in range(count)] for b in some]

    def add(slot, value):
        sums[slot * 8 : slot * 8 + 8] += value

    def put(table, at, value):
        table[at] = value if table[at] is None else table[at] + value

    def advance(vectors, images):
        level = []
        for b in some:
            level.append([])
            for x, h in zip(vectors[b], images[b]):
                level[b] += [SCALE * x - (SCALE * inverses[b]) * h, inverses[b] * x]
        return level

    images = apply([[start] for start in starts])
    zeroth = [[start.astype(jnp.float32)] for start in starts]
    for b in some:
        add(N0, fold(zeroth[b][0] * zeroth[b][0]))
        add(E0, fold(zeroth[b][0] * images[b][0]))
    first = advance(zeroth, images)

    images = apply([[split(x) for x in vectors] for vectors in first])
    for b in some:
        for m in range(2):
            for n in range(2):
                if m <= n:
                    add(N1 + m + n, (1.0 if m == n else 2.0) * fold(first[b][m] * first[b][n]))
                add(E1 + m + n, fold(first[b][m] * images[b][n]))
    second = advance(first, images)

    images = apply([[split(x) for x in vectors] for vectors in second])
    third = advance(second, images)
    for b in some:
        for m in range(8):
            basis_ref[m, slots[b]] = third[b][m]
        norm, energy, last = [None] * 9, [None] * 9, [None] * 27
        for m in range(4):
            for n in range(4):
                a0, a1 = POWERS[m][0] + POWERS[n][0], POWERS[m][1] + POWERS[n][1]
                put(energy, 3 * a0 + a1, fold(second[b][m] * images[b][n]))
                if m <= n:
                    put(norm, 3 * a0 + a1, (1.0 if m == n else 2.0) * fold(second[b][m] * second[b][n]))
                for d in range(2):
                    for e in range(2):
                        if (m, d) <= (n, e):
                            scale = 1.0 if (m, d) == (n, e) else 2.0
                            put(last, 9 * a0 + 3 * a1 + d + e, scale * fold(third[b][2 * m + d] * third[b][2 * n + e]))
        for at in range(9):
            add(N2 + at, norm[at])
            add(E2 + at, energy[at])
        for at in range(27):
            add(N3 + at, last[at])


def each_group(groups, body):
    if groups == 1:
        body(0)
    else:
        pl.loop(0, groups)(body)


def prepare_kernel(plan, sizes_hbm, psi_hbm, pre_hbm, *refs):
    own_refs, refs = refs[: plan.owners], refs[plan.owners :]
    own_cat, start_ref, inverse_ref, sizes_ref, psi_ref, pre_ref, sems = refs
    width = psi_ref.shape[-1]
    row = lax.axis_index("sector")
    core = row % 2
    chip = plan.first_chip(lax.axis_index("term"), row // 2)
    blocks = pl.ds(2 * chip, psi_ref.shape[0])
    copies = [
        pltpu.make_async_copy(sizes_hbm, sizes_ref, sems.at[0]),
        pltpu.make_async_copy(psi_hbm.at[blocks], psi_ref, sems.at[1]),
        pltpu.make_async_copy(pre_hbm.at[blocks], pre_ref, sems.at[2]),
    ]
    for copy in copies:
        copy.start()
    each_group(plan.groups, lambda g: stack_right(plan, own_cat.at[g], own_refs, g, psi_ref.shape[-1]))
    for copy in copies:
        copy.wait()
    row_ids = lax.broadcasted_iota(jnp.int32, (width, width), 0)
    col_ids = lax.broadcasted_iota(jnp.int32, (width, width), 1)

    def body(g):
        for b in range(2):
            block = 2 * g + (core if b == 0 else 1 - core)
            valid = (row_ids < sizes_ref[row]) & (col_ids < sizes_ref[2 * chip + block])
            start_ref[b, g] = jnp.where(valid, psi_ref[block].astype(jnp.float32), 0.0).astype(jnp.bfloat16)
            inverse_ref[b, g] = jnp.where(valid, 1.0 / pre_ref[block].astype(jnp.float32), 0.0)

    each_group(plan.groups, body)


def join_kernel(own_hbm, *refs):
    held_refs, out_ref, sem = refs[:-2], refs[-2], refs[-1]
    base = own_hbm.shape[0]
    copy = pltpu.make_async_copy(own_hbm, out_ref.at[:base], sem)
    copy.start()
    for ref in held_refs:
        out_ref[base : base + ref.shape[0]] = ref[...]
        base += ref.shape[0]
    copy.wait()


def join(own, *held):
    rows = own.shape[0] + sum(x.shape[0] for x in held)
    vmem = pl.BlockSpec(memory_space=pltpu.VMEM)
    return pl.pallas_call(
        join_kernel,
        out_shape=jax.ShapeDtypeStruct((rows,) + own.shape[1:], own.dtype),
        in_specs=[pl.BlockSpec(memory_space=pltpu.HBM)] + [vmem] * len(held),
        out_specs=vmem,
        scratch_shapes=[pltpu.SemaphoreType.DMA],
        compiler_params=pltpu.CompilerParams(vmem_limit_bytes=16 << 20),
        name="join",
    )(pltpu.with_memory_space_constraint(own, pltpu.HBM), *held)


def levels_kernel(plan, pieces, own_cat, start_ref, inverse_ref, *refs):
    left_refs, swap_refs, refs = refs[:pieces], refs[pieces : pieces + plan.owners], refs[pieces + plan.owners :]
    gram_ref, basis_ref, left_cat, swap_cat, sums = refs
    width = left_cat.shape[0]
    sums[...] = jnp.zeros_like(sums)
    for k, (ref, at) in enumerate((ref, at) for ref in left_refs for at in range(ref.shape[0])):
        left_cat[:, k * width : (k + 1) * width] = ref[at]

    def body(g):
        stack_right(plan, swap_cat, swap_refs, g, width)
        starts = [start_ref[b, g] for b in range(2)]
        inverses = [inverse_ref[b, g] for b in range(2)]
        levels(left_cat, (own_cat.at[g], swap_cat), sums, basis_ref, (2 * g, 2 * g + 1), starts, inverses)

    each_group(plan.groups, body)
    folded = functools.reduce(lambda a, b: a + b, [sums[pl.ds(s, ROWS, stride=8), :] for s in range(8)])
    totals = jnp.sum(folded, axis=1, keepdims=True)
    row_ids = lax.broadcasted_iota(jnp.int32, (ROWS, LANES), 0)
    col_ids = lax.broadcasted_iota(jnp.int32, (ROWS, LANES), 1)
    line = jnp.sum(jnp.where(row_ids == col_ids, totals, 0.0), axis=0, keepdims=True)
    gram_ref[...] = jnp.broadcast_to(line, gram_ref.shape)


def finish_kernel(count, gram_ref, basis_ref, out_ref, energy_ref):
    core = lax.axis_index("sector") % 2
    share = out_ref.shape[0]
    gram = jnp.sum(gram_ref[...], axis=0, keepdims=True)
    lane = lax.broadcasted_iota(jnp.int32, (1, LANES), 1)

    def total(base, size, weight):
        inside = (lane >= base) & (lane < base + size)
        return jnp.sum(jnp.where(inside, gram * weight, 0.0), axis=1, keepdims=True)

    def power(exponent, value):
        return jnp.where(exponent == 0, 1.0, jnp.where(exponent == 1, value, value * value))

    theta0 = total(E0, 1, 1.0) / total(N0, 1, 1.0)
    tau0 = SCALE * theta0
    norm1 = total(N1, 3, power(lane - N1, tau0))
    theta1 = total(E1, 3, power(lane - E1, tau0)) / norm1
    tau1 = SCALE * theta1

    def weight2(base):
        at = lane - base
        return power(at // 3, tau0) * power(at % 3, tau1)

    norm2 = total(N2, 9, weight2(N2))
    theta2 = total(E2, 9, weight2(E2)) / norm2
    tau2 = SCALE * theta2
    at = lane - N3
    norm3 = total(N3, 27, power(at // 9, tau0) * power(at // 3 % 3, tau1) * power(at % 3, tau2))

    def factor(gain, norm):
        return lax.rsqrt(gain * gain * jnp.maximum(norm, 0.0) / count + EPS)

    gain = jnp.full((1, 1), UNSCALE, jnp.float32)
    gain = factor(gain, norm1) * gain * UNSCALE
    gain = factor(gain, norm2) * gain * UNSCALE
    gain = factor(gain, norm3) * gain
    weights = [gain, gain * tau1, gain * tau0, gain * tau0 * tau1]
    for at in range(share):
        even = at % 2 == 0
        value = None
        for m in range(4):
            part = weights[m] * (basis_ref[2 * m, at] + tau2 * basis_ref[2 * m + 1, at])
            value = part if value is None else value + part
        block = (at // 2) * 2 + (core if even else 1 - core)
        out_ref[block] = value.astype(jnp.bfloat16)
    energy_ref[...] = jnp.where(lane == 0, theta0, jnp.where(lane == 1, theta1, theta2))


def assemble_kernel(plan, *refs):
    pieces, out_ref, sems = refs[: plan.owners], refs[plan.owners], refs[plan.owners + 1]
    share = pieces[0].shape[0]
    term, chip = lax.axis_index("term"), lax.axis_index("sector") // 2
    copies = []
    for at, m in enumerate(plan.last):
        first = plan.first_chip(plan.hop(term, m), chip) * 2
        copies.append(pltpu.make_async_copy(pieces[at], out_ref.at[pl.ds(first, share)], sems.at[at]))
        copies[-1].start()
    for copy in copies:
        copy.wait()


class Plan:
    def __init__(self, owners, sectors):
        self.owners, self.sectors, self.chips = owners, sectors, sectors // 2
        self.groups = self.chips // owners
        self.direct = self.groups == 1 and owners > 1 and owners & (owners - 1) == 0
        self.bits = [1 << b for b in reversed(range(owners.bit_length() - 1))]
        self.order = (0, 2, 3, 1) if self.direct and owners == 4 else tuple(range(owners))
        self.last = (0, 2, 1, 3) if owners == 4 else tuple(range(owners))
        offsets = [0]
        for bit in self.bits if self.direct else []:
            offsets = offsets + [offset ^ bit for offset in offsets]
        self.places = [self.order.index(offset) for offset in offsets] if self.direct else self.order
        if owners == 4:
            self.spread = ((1, 0, 3, 2), (0, 2, 1, 3), (2, 3, 0, 1), (3, 1, 2, 0))
        else:
            self.spread = tuple(tuple((q + t) % owners for q in range(owners)) for t in range(owners))

    def hop(self, term, offset):
        if self.owners & (self.owners - 1) == 0:
            return term ^ offset
        return (term + offset) % self.owners

    def back(self, offset):
        if self.owners & (self.owners - 1) == 0:
            return offset
        return (self.owners - offset) % self.owners

    def first_chip(self, term, chip):
        if not self.direct:
            return term * self.groups
        found = jnp.int32(0)
        for t in range(self.owners):
            for q in range(self.owners):
                hit = (term == t) & (chip == self.spread[t][q])
                found = jnp.where(hit, q, found)
        return found


def from_owner(plan, value, offset):
    if offset == 0:
        return value
    moves = [(plan.hop(t, offset), t) for t in range(plan.owners)]
    return lax.ppermute(value, "term", moves)


def inputs(plan, left, right):
    sectors, owners, groups = plan.sectors, plan.owners, plan.groups
    cores = [(i, i ^ 1) for i in range(sectors)]
    if plan.direct:
        lefts, held = [left], []
        for bit in plan.bits:
            lefts = [join(left, *held) if held else left]
            held.append(from_owner(plan, lefts[0], bit))
        lefts.append(held[-1])
        own = {}
        for m in plan.order:
            moves = []
            for t in range(owners):
                for q in range(plan.chips):
                    for c in range(2):
                        source = plan.hop(t, m) * sectors + 2 * q + c
                        moves.append((source, t * sectors + 2 * plan.spread[t][q] + c))
            own[m] = lax.ppermute(right, ("term", "sector"), moves)[None]
        own = [own[m] for m in plan.order]
        swapped = [lax.ppermute(x, "sector", cores) for x in own]
        return lefts, own, swapped
    everything = lax.all_gather(right, "sector").reshape((owners, groups, 2) + right.shape)
    by_chip = lax.dynamic_index_in_dim(everything, lax.axis_index("sector") % 2, 2, keepdims=False)
    spread_left = jnp.broadcast_to(left, (owners, 1) + left.shape)
    got = lax.all_to_all(jnp.concatenate([by_chip, spread_left], axis=1), "term", 0, 0)
    swapped = lax.ppermute(got[:, :groups], "sector", cores)
    lefts = [got[t, groups] for t in range(owners)]
    own = [got[t, :groups] for t in range(owners)]
    return lefts, own, [swapped[t] for t in range(owners)]


def local(plan, psi, left_env, right_env, precond, block_sizes):
    owners, sectors = plan.owners, plan.sectors
    devices = owners * sectors
    depth, width = right_env.shape[0], right_env.shape[-1]
    share = 2 * plan.groups
    lefts, own, swapped = inputs(plan, left_env[:, 0], right_env[:, 0])
    pieces = len(lefts)

    anywhere = pl.BlockSpec(memory_space=pltpu.HBM)
    vmem = pl.BlockSpec(memory_space=pltpu.VMEM)
    parked = [pltpu.with_memory_space_constraint(x, pltpu.HBM) for x in (block_sizes, psi[0], precond[0])]
    terms, groups = owners * depth, plan.groups
    params = pltpu.CompilerParams(vmem_limit_bytes=32 << 20)
    prepared = pl.pallas_call(
        functools.partial(prepare_kernel, plan),
        out_shape=(
            jax.ShapeDtypeStruct((groups, terms * width, 2 * width), jnp.bfloat16),
            jax.ShapeDtypeStruct((2, groups, width, width), jnp.bfloat16),
            jax.ShapeDtypeStruct((2, groups, width, width), jnp.float32),
        ),
        in_specs=[anywhere] * 3 + [vmem] * owners,
        out_specs=(vmem,) * 3,
        scratch_shapes=[
            pltpu.SMEM((sectors,), jnp.int32),
            pltpu.VMEM((share, width, width), jnp.bfloat16),
            pltpu.VMEM((share, width, width), jnp.bfloat16),
            pltpu.SemaphoreType.DMA((3,)),
        ],
        compiler_params=params,
        name="prepare",
    )(*parked, *own)
    gram, basis = pl.pallas_call(
        functools.partial(levels_kernel, plan, pieces),
        out_shape=(
            jax.ShapeDtypeStruct((devices, LANES), jnp.float32),
            jax.ShapeDtypeStruct((8, share, width, width), jnp.float32),
        ),
        in_specs=[vmem] * (3 + pieces + owners),
        out_specs=(vmem, vmem),
        scratch_shapes=[
            pltpu.VMEM((width, terms * width), jnp.bfloat16),
            pltpu.VMEM((terms * width, 2 * width), jnp.bfloat16),
            pltpu.VMEM((ROWS * 8, LANES), jnp.float32),
        ],
        compiler_params=params,
        name="levels",
    )(*prepared, *lefts, *swapped)
    gram = lax.all_to_all(gram, ("term", "sector"), 0, 0, tiled=True)
    count = float(sectors * sectors * width * width)
    blocks, energy = pl.pallas_call(
        functools.partial(finish_kernel, count),
        out_shape=(
            jax.ShapeDtypeStruct((share, width, width), jnp.bfloat16),
            jax.ShapeDtypeStruct((1, LANES), jnp.float32),
        ),
        in_specs=[vmem, vmem],
        out_specs=(vmem, vmem),
        compiler_params=params,
        name="finish",
    )(gram, basis)
    state = pl.pallas_call(
        functools.partial(assemble_kernel, plan),
        out_shape=jax.ShapeDtypeStruct((sectors, width, width), jnp.bfloat16),
        in_specs=[vmem] * owners,
        out_specs=anywhere,
        scratch_shapes=[pltpu.SemaphoreType.DMA((owners,))],
        compiler_params=pltpu.CompilerParams(vmem_limit_bytes=16 << 20),
        name="assemble",
    )(*[from_owner(plan, blocks, m) for m in plan.last])
    return (state[None], energy[0, :3])


def solution(mesh):
    in_specs = (
        P("sector", None, None, None),
        P("term", "sector", None, None),
        P("term", "sector", None, None),
        P("sector", None, None, None),
        P(),
    )
    out_specs = (P("sector", None, None, None), P())
    return jax.shard_map(
        functools.partial(local, Plan(mesh.shape["term"], mesh.shape["sector"])),
        mesh=mesh,
        in_specs=in_specs,
        out_specs=out_specs,
        check_vma=False,
    )
```

```python
import functools

import jax
import jax.numpy as jnp
from jax import lax
from jax.experimental import pallas as pl
from jax.experimental.pallas import tpu as pltpu
from jax.sharding import PartitionSpec as P

EPS = 1e-06
SCALE = 2.0**-12
UNSCALE = 2.0**12
ROWS = 64
LANES = 128

POWERS = ((0, 0), (0, 1), (1, 0), (1, 1))
N0, E0 = 0, 1
N1, E1 = 2, 5
N2, E2 = 8, 17
N3 = 26


def split(x):
    high = x.astype(jnp.bfloat16)
    low = (x - high.astype(jnp.float32)).astype(jnp.bfloat16)
    return jnp.concatenate([high, low], axis=1)


def fold(x):
    return functools.reduce(lambda a, b: a + b, [x[r : r + 8] for r in range(0, x.shape[0], 8)])


def stack_right(plan, right_cat, right_refs, g, width):
    depth = right_refs[0].shape[1]
    for k in range(plan.owners * depth):
        rows, ref = slice(k * width, (k + 1) * width), right_refs[plan.places[k // depth]]
        for half in range(2):
            right_cat[rows, half * width : (half + 1) * width] = ref[g, k % depth]


def levels(left_cat, right_cats, sums, basis_ref, slots, starts, inverses):
    width = starts[0].shape[0]
    terms = left_cat.shape[1] // width
    some = range(len(starts))

    def apply(vectors):
        columns = []
        for b in some:
            stacked = jnp.concatenate(vectors[b], axis=0)
            images = lax.dot_general(
                stacked,
                right_cats[b][:, : stacked.shape[1]],
                (((1,), (1,)), ((), ())),
                preferred_element_type=jnp.float32,
            ).astype(jnp.bfloat16)
            for n in range(len(vectors[b])):
                rows = images[n * width : (n + 1) * width]
                columns.append(jnp.concatenate([rows[:, k * width : (k + 1) * width] for k in range(terms)], axis=0))
        out = jnp.dot(left_cat[...], jnp.concatenate(columns, axis=1), preferred_element_type=jnp.float32)
        count = len(vectors[0])
        return [[out[:, (b * count + n) * width : (b * count + n + 1) * width] for n in range(count)] for b in some]

    def add(slot, value):
        sums[slot * 8 : slot * 8 + 8] += value

    def put(table, at, value):
        table[at] = value if table[at] is None else table[at] + value

    def advance(vectors, images):
        level = []
        for b in some:
            level.append([])
            for x, h in zip(vectors[b], images[b]):
                level[b] += [SCALE * x - (SCALE * inverses[b]) * h, inverses[b] * x]
        return level

    images = apply([[start] for start in starts])
    zeroth = [[start.astype(jnp.float32)] for start in starts]
    for b in some:
        add(N0, fold(zeroth[b][0] * zeroth[b][0]))
        add(E0, fold(zeroth[b][0] * images[b][0]))
    first = advance(zeroth, images)

    images = apply([[split(x) for x in vectors] for vectors in first])
    for b in some:
        for m in range(2):
            for n in range(2):
                if m <= n:
                    add(N1 + m + n, (1.0 if m == n else 2.0) * fold(first[b][m] * first[b][n]))
                add(E1 + m + n, fold(first[b][m] * images[b][n]))
    second = advance(first, images)

    images = apply([[split(x) for x in vectors] for vectors in second])
    third = advance(second, images)
    for b in some:
        for m in range(8):
            basis_ref[m, slots[b]] = third[b][m]
        norm, energy, last = [None] * 9, [None] * 9, [None] * 27
        for m in range(4):
            for n in range(4):
                a0, a1 = POWERS[m][0] + POWERS[n][0], POWERS[m][1] + POWERS[n][1]
                put(energy, 3 * a0 + a1, fold(second[b][m] * images[b][n]))
                if m <= n:
                    put(norm, 3 * a0 + a1, (1.0 if m == n else 2.0) * fold(second[b][m] * second[b][n]))
                for d in range(2):
                    for e in range(2):
                        if (m, d) <= (n, e):
                            scale = 1.0 if (m, d) == (n, e) else 2.0
                            put(last, 9 * a0 + 3 * a1 + d + e, scale * fold(third[b][2 * m + d] * third[b][2 * n + e]))
        for at in range(9):
            add(N2 + at, norm[at])
            add(E2 + at, energy[at])
        for at in range(27):
            add(N3 + at, last[at])


def each_group(groups, body):
    if groups == 1:
        body(0)
    else:
        pl.loop(0, groups)(body)


def stage_kernel(plan, sizes_hbm, psi_hbm, pre_hbm, left_hbm, *refs):
    held_refs, refs = refs[:-8], refs[-8:]
    left_ref, start_ref, inverse_ref, sizes_ref, psi_ref, pre_ref, own_ref, sems = refs
    width = psi_ref.shape[-1]
    row = lax.axis_index("sector")
    core = row % 2
    chip = plan.first_chip(lax.axis_index("term"), row // 2)
    blocks = pl.ds(2 * chip, psi_ref.shape[0])
    copies = [
        pltpu.make_async_copy(sizes_hbm, sizes_ref, sems.at[0]),
        pltpu.make_async_copy(psi_hbm.at[blocks], psi_ref, sems.at[1]),
        pltpu.make_async_copy(pre_hbm.at[blocks], pre_ref, sems.at[2]),
        pltpu.make_async_copy(left_hbm, own_ref, sems.at[3]),
    ]
    for copy in copies:
        copy.start()
    base = own_ref.shape[0]
    for ref in held_refs:
        left_ref[base : base + ref.shape[0]] = ref[...]
        base += ref.shape[0]
    for copy in copies:
        copy.wait()
    left_ref[: own_ref.shape[0]] = own_ref[...]
    row_ids = lax.broadcasted_iota(jnp.int32, (width, width), 0)
    col_ids = lax.broadcasted_iota(jnp.int32, (width, width), 1)

    def body(g):
        for b in range(2):
            block = 2 * g + (core if b == 0 else 1 - core)
            valid = (row_ids < sizes_ref[row]) & (col_ids < sizes_ref[2 * chip + block])
            start_ref[b, g] = jnp.where(valid, psi_ref[block].astype(jnp.float32), 0.0).astype(jnp.bfloat16)
            inverse_ref[b, g] = jnp.where(valid, 1.0 / pre_ref[block].astype(jnp.float32), 0.0)

    each_group(plan.groups, body)


def stack_kernel(plan, *refs):
    own_refs, own_cat = refs[: plan.owners], refs[plan.owners]
    each_group(plan.groups, lambda g: stack_right(plan, own_cat.at[g], own_refs, g, own_refs[0].shape[-1]))


def levels_kernel(plan, pieces, own_cat, start_ref, inverse_ref, *refs):
    left_refs, swap_refs, refs = refs[:pieces], refs[pieces : pieces + plan.owners], refs[pieces + plan.owners :]
    gram_ref, basis_ref, left_cat, swap_cat, sums = refs
    width = left_cat.shape[0]
    sums[...] = jnp.zeros_like(sums)
    for k, (ref, at) in enumerate((ref, at) for ref in left_refs for at in range(ref.shape[0])):
        left_cat[:, k * width : (k + 1) * width] = ref[at]

    def body(g):
        stack_right(plan, swap_cat, swap_refs, g, width)
        starts = [start_ref[b, g] for b in range(2)]
        inverses = [inverse_ref[b, g] for b in range(2)]
        levels(left_cat, (own_cat.at[g], swap_cat), sums, basis_ref, (2 * g, 2 * g + 1), starts, inverses)

    each_group(plan.groups, body)
    folded = functools.reduce(lambda a, b: a + b, [sums[pl.ds(s, ROWS, stride=8), :] for s in range(8)])
    totals = jnp.sum(folded, axis=1, keepdims=True)
    row_ids = lax.broadcasted_iota(jnp.int32, (ROWS, LANES), 0)
    col_ids = lax.broadcasted_iota(jnp.int32, (ROWS, LANES), 1)
    line = jnp.sum(jnp.where(row_ids == col_ids, totals, 0.0), axis=0, keepdims=True)
    gram_ref[...] = jnp.broadcast_to(line, gram_ref.shape)


def finish_kernel(count, gram_ref, basis_ref, out_ref, energy_ref):
    core = lax.axis_index("sector") % 2
    share = out_ref.shape[0]
    gram = jnp.sum(gram_ref[...], axis=0, keepdims=True)
    lane = lax.broadcasted_iota(jnp.int32, (1, LANES), 1)

    def total(base, size, weight):
        inside = (lane >= base) & (lane < base + size)
        return jnp.sum(jnp.where(inside, gram * weight, 0.0), axis=1, keepdims=True)

    def power(exponent, value):
        return jnp.where(exponent == 0, 1.0, jnp.where(exponent == 1, value, value * value))

    theta0 = total(E0, 1, 1.0) / total(N0, 1, 1.0)
    tau0 = SCALE * theta0
    norm1 = total(N1, 3, power(lane - N1, tau0))
    theta1 = total(E1, 3, power(lane - E1, tau0)) / norm1
    tau1 = SCALE * theta1

    def weight2(base):
        at = lane - base
        return power(at // 3, tau0) * power(at % 3, tau1)

    norm2 = total(N2, 9, weight2(N2))
    theta2 = total(E2, 9, weight2(E2)) / norm2
    tau2 = SCALE * theta2
    at = lane - N3
    norm3 = total(N3, 27, power(at // 9, tau0) * power(at // 3 % 3, tau1) * power(at % 3, tau2))

    def factor(gain, norm):
        return lax.rsqrt(gain * gain * jnp.maximum(norm, 0.0) / count + EPS)

    gain = jnp.full((1, 1), UNSCALE, jnp.float32)
    gain = factor(gain, norm1) * gain * UNSCALE
    gain = factor(gain, norm2) * gain * UNSCALE
    gain = factor(gain, norm3) * gain
    weights = [gain, gain * tau1, gain * tau0, gain * tau0 * tau1]
    for at in range(share):
        even = at % 2 == 0
        value = None
        for m in range(4):
            part = weights[m] * (basis_ref[2 * m, at] + tau2 * basis_ref[2 * m + 1, at])
            value = part if value is None else value + part
        block = (at // 2) * 2 + (core if even else 1 - core)
        out_ref[block] = value.astype(jnp.bfloat16)
    energy_ref[...] = jnp.where(lane == 0, theta0, jnp.where(lane == 1, theta1, theta2))


def assemble_kernel(plan, *refs):
    pieces, out_ref, sems = refs[: plan.owners], refs[plan.owners], refs[plan.owners + 1]
    share = pieces[0].shape[0]
    term, chip = lax.axis_index("term"), lax.axis_index("sector") // 2
    copies = []
    for m in range(plan.owners):
        first = plan.first_chip(plan.hop(term, m), chip) * 2
        copies.append(pltpu.make_async_copy(pieces[m], out_ref.at[pl.ds(first, share)], sems.at[m]))
        copies[-1].start()
    for copy in copies:
        copy.wait()


class Plan:
    def __init__(self, owners, sectors):
        self.owners, self.sectors, self.chips = owners, sectors, sectors // 2
        self.groups = self.chips // owners
        self.direct = self.groups == 1 and owners > 1 and owners & (owners - 1) == 0
        self.bits = [1 << b for b in reversed(range(owners.bit_length() - 1))]
        self.order = (0, 2, 3, 1) if self.direct and owners == 4 else tuple(range(owners))
        offsets = [0]
        for bit in self.bits if self.direct else []:
            offsets = offsets + [offset ^ bit for offset in offsets]
        self.places = [self.order.index(offset) for offset in offsets] if self.direct else self.order
        if owners == 4:
            self.spread = ((1, 0, 3, 2), (0, 2, 1, 3), (2, 3, 0, 1), (3, 1, 2, 0))
        else:
            self.spread = tuple(tuple((q + t) % owners for q in range(owners)) for t in range(owners))

    def hop(self, term, offset):
        if self.owners & (self.owners - 1) == 0:
            return term ^ offset
        return (term + offset) % self.owners

    def back(self, offset):
        if self.owners & (self.owners - 1) == 0:
            return offset
        return (self.owners - offset) % self.owners

    def first_chip(self, term, chip):
        if not self.direct:
            return term * self.groups
        found = jnp.int32(0)
        for t in range(self.owners):
            for q in range(self.owners):
                hit = (term == t) & (chip == self.spread[t][q])
                found = jnp.where(hit, q, found)
        return found


def from_owner(plan, value, offset):
    if offset == 0:
        return value
    moves = [(plan.hop(t, offset), t) for t in range(plan.owners)]
    return lax.ppermute(value, "term", moves)


def inputs(plan, left, right, stage):
    sectors, owners, groups = plan.sectors, plan.owners, plan.groups
    cores = [(i, i ^ 1) for i in range(sectors)]
    if plan.direct:
        held = [left]
        for bit in plan.bits[:-1]:
            held.append(from_owner(plan, jnp.concatenate(held, axis=0), bit))
        left, *prepared = stage(left, held[1:])
        lefts = [left, from_owner(plan, left, plan.bits[-1])]
        own = {}
        for m in plan.order:
            moves = []
            for t in range(owners):
                for q in range(plan.chips):
                    for c in range(2):
                        source = plan.hop(t, m) * sectors + 2 * q + c
                        moves.append((source, t * sectors + 2 * plan.spread[t][q] + c))
            own[m] = lax.ppermute(right, ("term", "sector"), moves)[None]
        own = [own[m] for m in plan.order]
        swapped = [lax.ppermute(x, "sector", cores) for x in own]
        return lefts, own, swapped, prepared
    left, *prepared = stage(left, [])
    everything = lax.all_gather(right, "sector").reshape((owners, groups, 2) + right.shape)
    by_chip = lax.dynamic_index_in_dim(everything, lax.axis_index("sector") % 2, 2, keepdims=False)
    spread_left = jnp.broadcast_to(left, (owners, 1) + left.shape)
    got = lax.all_to_all(jnp.concatenate([by_chip, spread_left], axis=1), "term", 0, 0)
    swapped = lax.ppermute(got[:, :groups], "sector", cores)
    lefts = [got[t, groups] for t in range(owners)]
    own = [got[t, :groups] for t in range(owners)]
    return lefts, own, [swapped[t] for t in range(owners)], prepared


def local(plan, psi, left_env, right_env, precond, block_sizes):
    owners, sectors = plan.owners, plan.sectors
    devices = owners * sectors
    depth, width = right_env.shape[0], right_env.shape[-1]
    share = 2 * plan.groups

    anywhere = pl.BlockSpec(memory_space=pltpu.HBM)
    vmem = pl.BlockSpec(memory_space=pltpu.VMEM)
    terms, groups = owners * depth, plan.groups
    params = pltpu.CompilerParams(vmem_limit_bytes=32 << 20)

    def stage(left, held):
        rows = depth + sum(x.shape[0] for x in held)
        parked = [pltpu.with_memory_space_constraint(x, pltpu.HBM) for x in (block_sizes, psi[0], precond[0], left)]
        return pl.pallas_call(
            functools.partial(stage_kernel, plan),
            out_shape=(
                jax.ShapeDtypeStruct((rows, width, width), jnp.bfloat16),
                jax.ShapeDtypeStruct((2, groups, width, width), jnp.bfloat16),
                jax.ShapeDtypeStruct((2, groups, width, width), jnp.float32),
            ),
            in_specs=[anywhere] * 4 + [vmem] * len(held),
            out_specs=(vmem,) * 3,
            scratch_shapes=[
                pltpu.SMEM((sectors,), jnp.int32),
                pltpu.VMEM((share, width, width), jnp.bfloat16),
                pltpu.VMEM((share, width, width), jnp.bfloat16),
                pltpu.VMEM((depth, width, width), jnp.bfloat16),
                pltpu.SemaphoreType.DMA((4,)),
            ],
            compiler_params=params,
            name="stage",
        )(*parked, *held)

    lefts, own, swapped, prepared = inputs(plan, left_env[:, 0], right_env[:, 0], stage)
    pieces = len(lefts)
    own_cat = pl.pallas_call(
        functools.partial(stack_kernel, plan),
        out_shape=jax.ShapeDtypeStruct((groups, terms * width, 2 * width), jnp.bfloat16),
        in_specs=[vmem] * owners,
        out_specs=vmem,
        compiler_params=params,
        name="stack",
    )(*own)
    gram, basis = pl.pallas_call(
        functools.partial(levels_kernel, plan, pieces),
        out_shape=(
            jax.ShapeDtypeStruct((devices, LANES), jnp.float32),
            jax.ShapeDtypeStruct((8, share, width, width), jnp.float32),
        ),
        in_specs=[vmem] * (3 + pieces + owners),
        out_specs=(vmem, vmem),
        scratch_shapes=[
            pltpu.VMEM((width, terms * width), jnp.bfloat16),
            pltpu.VMEM((terms * width, 2 * width), jnp.bfloat16),
            pltpu.VMEM((ROWS * 8, LANES), jnp.float32),
        ],
        compiler_params=params,
        name="levels",
    )(own_cat, *prepared, *lefts, *swapped)
    gram = lax.all_to_all(gram, ("term", "sector"), 0, 0, tiled=True)
    count = float(sectors * sectors * width * width)
    blocks, energy = pl.pallas_call(
        functools.partial(finish_kernel, count),
        out_shape=(
            jax.ShapeDtypeStruct((share, width, width), jnp.bfloat16),
            jax.ShapeDtypeStruct((1, LANES), jnp.float32),
        ),
        in_specs=[vmem, vmem],
        out_specs=(vmem, vmem),
        compiler_params=params,
        name="finish",
    )(gram, basis)
    state = pl.pallas_call(
        functools.partial(assemble_kernel, plan),
        out_shape=jax.ShapeDtypeStruct((sectors, width, width), jnp.bfloat16),
        in_specs=[vmem] * owners,
        out_specs=anywhere,
        scratch_shapes=[pltpu.SemaphoreType.DMA((owners,))],
        compiler_params=pltpu.CompilerParams(vmem_limit_bytes=16 << 20),
        name="assemble",
    )(*[from_owner(plan, blocks, m) for m in range(owners)])
    return (state[None], energy[0, :3])


def solution(mesh):
    in_specs = (
        P("sector", None, None, None),
        P("term", "sector", None, None),
        P("term", "sector", None, None),
        P("sector", None, None, None),
        P(),
    )
    out_specs = (P("sector", None, None, None), P())
    return jax.shard_map(
        functools.partial(local, Plan(mesh.shape["term"], mesh.shape["sector"])),
        mesh=mesh,
        in_specs=in_specs,
        out_specs=out_specs,
        check_vma=False,
    )
```

```python
import functools

import jax
import jax.numpy as jnp
from jax import lax
from jax.experimental import pallas as pl
from jax.experimental.pallas import tpu as pltpu
from jax.sharding import PartitionSpec as P

EPS = 1e-06
SCALE = 2.0**-12
UNSCALE = 2.0**12
ROWS = 64
LANES = 128

POWERS = ((0, 0), (0, 1), (1, 0), (1, 1))
N0, E0 = 0, 1
N1, E1 = 2, 5
N2, E2 = 8, 17
N3 = 26


def split(x):
    high = x.astype(jnp.bfloat16)
    low = (x - high.astype(jnp.float32)).astype(jnp.bfloat16)
    return jnp.concatenate([high, low], axis=1)


def fold(x):
    return functools.reduce(lambda a, b: a + b, [x[r : r + 8] for r in range(0, x.shape[0], 8)])


def stack_right(plan, right_cat, right_refs, g, width):
    depth = right_refs[0].shape[1]
    for k in range(plan.owners * depth):
        rows, ref = slice(k * width, (k + 1) * width), right_refs[plan.places[k // depth]]
        for half in range(2):
            right_cat[rows, half * width : (half + 1) * width] = ref[g, k % depth]


def levels(left_cat, right_cats, sums, basis_ref, slots, starts, inverses):
    width = starts[0].shape[0]
    terms = left_cat.shape[1] // width
    some = range(len(starts))

    def apply(vectors):
        columns = []
        for b in some:
            stacked = jnp.concatenate(vectors[b], axis=0)
            images = lax.dot_general(
                stacked,
                right_cats[b][:, : stacked.shape[1]],
                (((1,), (1,)), ((), ())),
                preferred_element_type=jnp.float32,
            ).astype(jnp.bfloat16)
            for n in range(len(vectors[b])):
                rows = images[n * width : (n + 1) * width]
                columns.append(jnp.concatenate([rows[:, k * width : (k + 1) * width] for k in range(terms)], axis=0))
        out = jnp.dot(left_cat[...], jnp.concatenate(columns, axis=1), preferred_element_type=jnp.float32)
        count = len(vectors[0])
        return [[out[:, (b * count + n) * width : (b * count + n + 1) * width] for n in range(count)] for b in some]

    def add(slot, value):
        sums[slot * 8 : slot * 8 + 8] += value

    def put(table, at, value):
        table[at] = value if table[at] is None else table[at] + value

    def advance(vectors, images):
        level = []
        for b in some:
            level.append([])
            for x, h in zip(vectors[b], images[b]):
                level[b] += [SCALE * x - (SCALE * inverses[b]) * h, inverses[b] * x]
        return level

    images = apply([[start] for start in starts])
    zeroth = [[start.astype(jnp.float32)] for start in starts]
    for b in some:
        add(N0, fold(zeroth[b][0] * zeroth[b][0]))
        add(E0, fold(zeroth[b][0] * images[b][0]))
    first = advance(zeroth, images)

    images = apply([[split(x) for x in vectors] for vectors in first])
    for b in some:
        for m in range(2):
            for n in range(2):
                if m <= n:
                    add(N1 + m + n, (1.0 if m == n else 2.0) * fold(first[b][m] * first[b][n]))
                add(E1 + m + n, fold(first[b][m] * images[b][n]))
    second = advance(first, images)

    images = apply([[split(x) for x in vectors] for vectors in second])
    third = advance(second, images)
    for b in some:
        for m in range(8):
            basis_ref[m, slots[b]] = third[b][m]
        norm, energy, last = [None] * 9, [None] * 9, [None] * 27
        for m in range(4):
            for n in range(4):
                a0, a1 = POWERS[m][0] + POWERS[n][0], POWERS[m][1] + POWERS[n][1]
                put(energy, 3 * a0 + a1, fold(second[b][m] * images[b][n]))
                if m <= n:
                    put(norm, 3 * a0 + a1, (1.0 if m == n else 2.0) * fold(second[b][m] * second[b][n]))
                for d in range(2):
                    for e in range(2):
                        if (m, d) <= (n, e):
                            scale = 1.0 if (m, d) == (n, e) else 2.0
                            put(last, 9 * a0 + 3 * a1 + d + e, scale * fold(third[b][2 * m + d] * third[b][2 * n + e]))
        for at in range(9):
            add(N2 + at, norm[at])
            add(E2 + at, energy[at])
        for at in range(27):
            add(N3 + at, last[at])


def each_group(groups, body):
    if groups == 1:
        body(0)
    else:
        pl.loop(0, groups)(body)


def prepare_kernel(plan, sizes_hbm, psi_hbm, pre_hbm, *refs):
    own_refs, refs = refs[: plan.owners], refs[plan.owners :]
    own_cat, start_ref, inverse_ref, sizes_ref, psi_ref, pre_ref, sems = refs
    width = psi_ref.shape[-1]
    row = lax.axis_index("sector")
    core = row % 2
    chip = plan.first_chip(lax.axis_index("term"), row // 2)
    blocks = pl.ds(2 * chip, psi_ref.shape[0])
    copies = [
        pltpu.make_async_copy(sizes_hbm, sizes_ref, sems.at[0]),
        pltpu.make_async_copy(psi_hbm.at[blocks], psi_ref, sems.at[1]),
        pltpu.make_async_copy(pre_hbm.at[blocks], pre_ref, sems.at[2]),
    ]
    for copy in copies:
        copy.start()
    each_group(plan.groups, lambda g: stack_right(plan, own_cat.at[g], own_refs, g, psi_ref.shape[-1]))
    for copy in copies:
        copy.wait()
    row_ids = lax.broadcasted_iota(jnp.int32, (width, width), 0)
    col_ids = lax.broadcasted_iota(jnp.int32, (width, width), 1)

    def body(g):
        for b in range(2):
            block = 2 * g + (core if b == 0 else 1 - core)
            valid = (row_ids < sizes_ref[row]) & (col_ids < sizes_ref[2 * chip + block])
            start_ref[b, g] = jnp.where(valid, psi_ref[block].astype(jnp.float32), 0.0).astype(jnp.bfloat16)
            inverse_ref[b, g] = jnp.where(valid, 1.0 / pre_ref[block].astype(jnp.float32), 0.0)

    each_group(plan.groups, body)


def join_kernel(own_hbm, *refs):
    held_refs, out_ref, sem = refs[:-2], refs[-2], refs[-1]
    base = own_hbm.shape[0]
    copy = pltpu.make_async_copy(own_hbm, out_ref.at[:base], sem)
    copy.start()
    for ref in held_refs:
        out_ref[base : base + ref.shape[0]] = ref[...]
        base += ref.shape[0]
    copy.wait()


def join(own, *held):
    rows = own.shape[0] + sum(x.shape[0] for x in held)
    vmem = pl.BlockSpec(memory_space=pltpu.VMEM)
    return pl.pallas_call(
        join_kernel,
        out_shape=jax.ShapeDtypeStruct((rows,) + own.shape[1:], own.dtype),
        in_specs=[pl.BlockSpec(memory_space=pltpu.HBM)] + [vmem] * len(held),
        out_specs=vmem,
        scratch_shapes=[pltpu.SemaphoreType.DMA],
        compiler_params=pltpu.CompilerParams(vmem_limit_bytes=16 << 20),
        name="join",
    )(pltpu.with_memory_space_constraint(own, pltpu.HBM), *held)


def levels_kernel(plan, pieces, own_cat, start_ref, inverse_ref, *refs):
    left_refs, swap_refs, refs = refs[:pieces], refs[pieces : pieces + plan.owners], refs[pieces + plan.owners :]
    gram_ref, basis_ref, left_cat, swap_cat, sums = refs
    width = left_cat.shape[0]
    sums[...] = jnp.zeros_like(sums)
    for k, (ref, at) in enumerate((ref, at) for ref in left_refs for at in range(ref.shape[0])):
        left_cat[:, k * width : (k + 1) * width] = ref[at]

    def body(g):
        stack_right(plan, swap_cat, swap_refs, g, width)
        starts = [start_ref[b, g] for b in range(2)]
        inverses = [inverse_ref[b, g] for b in range(2)]
        levels(left_cat, (own_cat.at[g], swap_cat), sums, basis_ref, (2 * g, 2 * g + 1), starts, inverses)

    each_group(plan.groups, body)
    folded = functools.reduce(lambda a, b: a + b, [sums[pl.ds(s, ROWS, stride=8), :] for s in range(8)])
    totals = jnp.sum(folded, axis=1, keepdims=True)
    row_ids = lax.broadcasted_iota(jnp.int32, (ROWS, LANES), 0)
    col_ids = lax.broadcasted_iota(jnp.int32, (ROWS, LANES), 1)
    line = jnp.sum(jnp.where(row_ids == col_ids, totals, 0.0), axis=0, keepdims=True)
    gram_ref[...] = jnp.broadcast_to(line, gram_ref.shape)


def finish_kernel(count, gram_ref, basis_ref, out_ref, energy_ref):
    core = lax.axis_index("sector") % 2
    share = out_ref.shape[0]
    gram = jnp.sum(gram_ref[...], axis=0, keepdims=True)
    lane = lax.broadcasted_iota(jnp.int32, (1, LANES), 1)

    def total(base, size, weight):
        inside = (lane >= base) & (lane < base + size)
        return jnp.sum(jnp.where(inside, gram * weight, 0.0), axis=1, keepdims=True)

    def power(exponent, value):
        return jnp.where(exponent == 0, 1.0, jnp.where(exponent == 1, value, value * value))

    theta0 = total(E0, 1, 1.0) / total(N0, 1, 1.0)
    tau0 = SCALE * theta0
    norm1 = total(N1, 3, power(lane - N1, tau0))
    theta1 = total(E1, 3, power(lane - E1, tau0)) / norm1
    tau1 = SCALE * theta1

    def weight2(base):
        at = lane - base
        return power(at // 3, tau0) * power(at % 3, tau1)

    norm2 = total(N2, 9, weight2(N2))
    theta2 = total(E2, 9, weight2(E2)) / norm2
    tau2 = SCALE * theta2
    at = lane - N3
    norm3 = total(N3, 27, power(at // 9, tau0) * power(at // 3 % 3, tau1) * power(at % 3, tau2))

    def factor(gain, norm):
        return lax.rsqrt(gain * gain * jnp.maximum(norm, 0.0) / count + EPS)

    gain = jnp.full((1, 1), UNSCALE, jnp.float32)
    gain = factor(gain, norm1) * gain * UNSCALE
    gain = factor(gain, norm2) * gain * UNSCALE
    gain = factor(gain, norm3) * gain
    weights = [gain, gain * tau1, gain * tau0, gain * tau0 * tau1]
    for at in range(share):
        even = at % 2 == 0
        value = None
        for m in range(4):
            part = weights[m] * (basis_ref[2 * m, at] + tau2 * basis_ref[2 * m + 1, at])
            value = part if value is None else value + part
        block = (at // 2) * 2 + (core if even else 1 - core)
        out_ref[block] = value.astype(jnp.bfloat16)
    energy_ref[...] = jnp.where(lane == 0, theta0, jnp.where(lane == 1, theta1, theta2))


def assemble_kernel(plan, *refs):
    pieces, out_ref, sems = refs[: plan.owners], refs[plan.owners], refs[plan.owners + 1]
    share = pieces[0].shape[0]
    term, chip = lax.axis_index("term"), lax.axis_index("sector") // 2
    copies = []
    for at, m in enumerate(plan.last):
        first = plan.first_chip(plan.hop(term, m), chip) * 2
        copies.append(pltpu.make_async_copy(pieces[at], out_ref.at[pl.ds(first, share)], sems.at[at]))
        copies[-1].start()
    for copy in copies:
        copy.wait()


class Plan:
    def __init__(self, owners, sectors):
        self.owners, self.sectors, self.chips = owners, sectors, sectors // 2
        self.groups = self.chips // owners
        self.direct = self.groups == 1 and owners > 1 and owners & (owners - 1) == 0
        self.bits = [1 << b for b in reversed(range(owners.bit_length() - 1))]
        self.order = (0, 3, 1, 2) if self.direct and owners == 4 else tuple(range(owners))
        self.last = (0, 2, 1, 3) if owners == 4 else tuple(range(owners))
        offsets = [0]
        for bit in self.bits if self.direct else []:
            offsets = offsets + [offset ^ bit for offset in offsets]
        self.places = [self.order.index(offset) for offset in offsets] if self.direct else self.order
        if owners == 4:
            self.spread = ((2, 3, 1, 0), (0, 1, 3, 2), (3, 2, 0, 1), (1, 0, 2, 3))
        else:
            self.spread = tuple(tuple((q + t) % owners for q in range(owners)) for t in range(owners))

    def hop(self, term, offset):
        if self.owners & (self.owners - 1) == 0:
            return term ^ offset
        return (term + offset) % self.owners

    def back(self, offset):
        if self.owners & (self.owners - 1) == 0:
            return offset
        return (self.owners - offset) % self.owners

    def first_chip(self, term, chip):
        if not self.direct:
            return term * self.groups
        found = jnp.int32(0)
        for t in range(self.owners):
            for q in range(self.owners):
                hit = (term == t) & (chip == self.spread[t][q])
                found = jnp.where(hit, q, found)
        return found


def from_owner(plan, value, offset):
    if offset == 0:
        return value
    moves = [(plan.hop(t, offset), t) for t in range(plan.owners)]
    return lax.ppermute(value, "term", moves)


def inputs(plan, left, right):
    sectors, owners, groups = plan.sectors, plan.owners, plan.groups
    cores = [(i, i ^ 1) for i in range(sectors)]
    if plan.direct:
        lefts, held = [left], []
        for bit in plan.bits:
            lefts = [join(left, *held) if held else left]
            held.append(from_owner(plan, lefts[0], bit))
        lefts.append(held[-1])
        own = {}
        for m in plan.order:
            moves = []
            for t in range(owners):
                for q in range(plan.chips):
                    for c in range(2):
                        source = plan.hop(t, m) * sectors + 2 * q + c
                        moves.append((source, t * sectors + 2 * plan.spread[t][q] + c))
            own[m] = lax.ppermute(right, ("term", "sector"), moves)[None]
        own = [own[m] for m in plan.order]
        swapped = [lax.ppermute(x, "sector", cores) for x in own]
        return lefts, own, swapped
    everything = lax.all_gather(right, "sector").reshape((owners, groups, 2) + right.shape)
    by_chip = lax.dynamic_index_in_dim(everything, lax.axis_index("sector") % 2, 2, keepdims=False)
    spread_left = jnp.broadcast_to(left, (owners, 1) + left.shape)
    got = lax.all_to_all(jnp.concatenate([by_chip, spread_left], axis=1), "term", 0, 0)
    swapped = lax.ppermute(got[:, :groups], "sector", cores)
    lefts = [got[t, groups] for t in range(owners)]
    own = [got[t, :groups] for t in range(owners)]
    return lefts, own, [swapped[t] for t in range(owners)]


def local(plan, psi, left_env, right_env, precond, block_sizes):
    owners, sectors = plan.owners, plan.sectors
    devices = owners * sectors
    depth, width = right_env.shape[0], right_env.shape[-1]
    share = 2 * plan.groups
    lefts, own, swapped = inputs(plan, left_env[:, 0], right_env[:, 0])
    pieces = len(lefts)

    anywhere = pl.BlockSpec(memory_space=pltpu.HBM)
    vmem = pl.BlockSpec(memory_space=pltpu.VMEM)
    parked = [pltpu.with_memory_space_constraint(x, pltpu.HBM) for x in (block_sizes, psi[0], precond[0])]
    terms, groups = owners * depth, plan.groups
    params = pltpu.CompilerParams(vmem_limit_bytes=32 << 20)
    prepared = pl.pallas_call(
        functools.partial(prepare_kernel, plan),
        out_shape=(
            jax.ShapeDtypeStruct((groups, terms * width, 2 * width), jnp.bfloat16),
            jax.ShapeDtypeStruct((2, groups, width, width), jnp.bfloat16),
            jax.ShapeDtypeStruct((2, groups, width, width), jnp.float32),
        ),
        in_specs=[anywhere] * 3 + [vmem] * owners,
        out_specs=(vmem,) * 3,
        scratch_shapes=[
            pltpu.SMEM((sectors,), jnp.int32),
            pltpu.VMEM((share, width, width), jnp.bfloat16),
            pltpu.VMEM((share, width, width), jnp.bfloat16),
            pltpu.SemaphoreType.DMA((3,)),
        ],
        compiler_params=params,
        name="prepare",
    )(*parked, *own)
    gram, basis = pl.pallas_call(
        functools.partial(levels_kernel, plan, pieces),
        out_shape=(
            jax.ShapeDtypeStruct((devices, LANES), jnp.float32),
            jax.ShapeDtypeStruct((8, share, width, width), jnp.float32),
        ),
        in_specs=[vmem] * (3 + pieces + owners),
        out_specs=(vmem, vmem),
        scratch_shapes=[
            pltpu.VMEM((width, terms * width), jnp.bfloat16),
            pltpu.VMEM((terms * width, 2 * width), jnp.bfloat16),
            pltpu.VMEM((ROWS * 8, LANES), jnp.float32),
        ],
        compiler_params=params,
        name="levels",
    )(*prepared, *lefts, *swapped)
    gram = lax.all_to_all(gram, ("term", "sector"), 0, 0, tiled=True)
    count = float(sectors * sectors * width * width)
    blocks, energy = pl.pallas_call(
        functools.partial(finish_kernel, count),
        out_shape=(
            jax.ShapeDtypeStruct((share, width, width), jnp.bfloat16),
            jax.ShapeDtypeStruct((1, LANES), jnp.float32),
        ),
        in_specs=[vmem, vmem],
        out_specs=(vmem, vmem),
        compiler_params=params,
        name="finish",
    )(gram, basis)
    state = pl.pallas_call(
        functools.partial(assemble_kernel, plan),
        out_shape=jax.ShapeDtypeStruct((sectors, width, width), jnp.bfloat16),
        in_specs=[vmem] * owners,
        out_specs=anywhere,
        scratch_shapes=[pltpu.SemaphoreType.DMA((owners,))],
        compiler_params=pltpu.CompilerParams(vmem_limit_bytes=16 << 20),
        name="assemble",
    )(*[from_owner(plan, blocks, m) for m in plan.last])
    return (state[None], energy[0, :3])


def solution(mesh):
    in_specs = (
        P("sector", None, None, None),
        P("term", "sector", None, None),
        P("term", "sector", None, None),
        P("sector", None, None, None),
        P(),
    )
    out_specs = (P("sector", None, None, None), P())
    return jax.shard_map(
        functools.partial(local, Plan(mesh.shape["term"], mesh.shape["sector"])),
        mesh=mesh,
        in_specs=in_specs,
        out_specs=out_specs,
        check_vma=False,
    )
```
